256 devices in a mesh: row: 16 (over z, core), col: 16 (over y, x).
Axes of the slice: x: 4, y: 4, z: 8, core: 2. Of those that a mesh axis runs over, the one named last changes fastest.
Arguments:
- diag_block: float32 [512, 512], P('row', 'col'), may hold values from 0 to 1.7, as said below
- panel: float32 [16384, 512], P('row', 'col'), may hold values from -0.6 to 0.6
- slab: float32 [16384, 16384], P('row', 'col'), may hold values from -6 to 6
Outputs:
- chol_factor: float32 [512, 512], P('row', 'col')
- panel_factor: float32 [16384, 512], P('row', 'col')
- slab_update: float32 [16384, 16384], P('row', 'col')
The draws below stay inside these ranges and needn't reach their ends.
Inputs may be any that keep to these rules, and one draw needn't show every extreme that they name: diag_block is symmetric positive definite, with smallest eigenvalue at least 0.3.
All inputs are finite; a program needn't handle non-finite values.
Results may differ from the reference program's by a relative error of at most 0.0003.
Values sent between devices are 32-bit elements; how exact they have to be, the bound alone decides.
A program may use at most 64 MiB of HBM per device.

```python
import jax
import jax.numpy as jnp
from jax import lax

NB = 512
ROWS = 16384
COLS = 16384


def draw_diag_block(key, part):
    first, second = jax.random.split(key, 2)
    points = 3.0 * jax.random.uniform(first, (4, NB), jnp.float32)
    apart0 = (points[0][:, None] - points[0][None, :]) ** 2
    apart1 = (points[1][:, None] - points[1][None, :]) ** 2
    apart2 = (points[2][:, None] - points[2][None, :]) ** 2
    apart3 = (points[3][:, None] - points[3][None, :]) ** 2
    squared = apart0 + apart1 + apart2 + apart3
    kernel = jnp.exp(-0.5 * squared)
    nugget = 0.3 + 0.4 * jax.random.uniform(second, (NB,), jnp.float32)
    identity = jnp.eye(NB, dtype=jnp.float32)
    return kernel + identity * nugget[None, :]


def block_scale(own_key, extent, shards, smallest, top_value):
    gain, own = 1.0, jax.random.fold_in(own_key, 6)
    for position, shards_of in shards:
        heights = jnp.exp(jax.random.uniform(jax.random.fold_in(own, position), (shards_of,), jnp.float32, smallest / len(shards), top_value / len(shards)))
        gain = gain * jnp.repeat(heights, extent[position] // shards_of).reshape([-1 if axis == position else 1 for axis in range(len(extent))])
    return gain


def bell_draw(stream_key, shape, spread, most, pieces=(), held_as=jnp.bfloat16):
    loudness = block_scale(stream_key, shape, pieces, -0.22, 0.18) if pieces else 1.0
    result = jax.random.normal(stream_key, shape, jnp.float32) * spread * loudness
    return jnp.minimum(jnp.maximum(result, -most), most).astype(held_as)


def setup_inputs(seed: int = 0) -> dict:
    streams_of = jax.random.split(jax.random.key(seed), 4)
    return {
        "diag_block": draw_diag_block(jax.random.fold_in(streams_of[3], 71), 0),
        "panel": bell_draw(streams_of[1], (ROWS, NB), 0.1, 0.6, ((0, 16), (1, 16)), jnp.float32),
        "slab": bell_draw(streams_of[2], (ROWS, COLS), 1.0, 6.0, ((0, 16), (1, 16)), jnp.float32),
    }


def reference(diag_block, panel, slab):
    factor = jnp.linalg.cholesky(diag_block)
    identity = jnp.eye(NB, dtype=diag_block.dtype)
    inverse = lax.linalg.triangular_solve(factor, identity, left_side=True, lower=True)
    solved = jnp.dot(panel, inverse.T, precision=lax.Precision.HIGHEST)
    width = slab.shape[1]
    update = slab - jnp.dot(solved, solved[:width].T, precision=lax.Precision.HIGHEST)
    return (factor, solved, update)
```

```python
import jax
import jax.numpy as jnp
from jax import lax
from jax.sharding import PartitionSpec as P
from jax.experimental import pallas as pl
from jax.experimental.pallas import tpu as pltpu
F=jnp.float32
NB=512; BLK=128

def split(x):
    hi=x.astype(jnp.bfloat16)
    lo=(x-hi.astype(F)).astype(jnp.bfloat16)
    return hi,lo
def dot3(a,b,dims):
    ah,al=split(a); bh,bl=split(b)
    d=lambda x,y: lax.dot_general(x,y,(dims,((),())),preferred_element_type=F)
    return d(ah,bh)+(d(ah,bl)+d(al,bh))
NN=((1,),(0,)); NT=((1,),(1,))

def sweep(tiles):
    lane=lax.broadcasted_iota(jnp.int32,(8,BLK),1)
    sub=lax.broadcasted_iota(jnp.int32,(8,BLK),0)
    n=len(tiles); out=[]
    tiles=list(tiles)
    for p in range(n):
        R=tiles[p]
        rows=[jnp.broadcast_to(R[k:k+1,:],(8,BLK)) for k in range(8)]
        B={(k,i):jnp.broadcast_to(rows[k][:,8*p+i:8*p+i+1],(8,BLK)) for k in range(8) for i in range(k,8)}
        inm=(lane>=8*p)&(lane<8*p+8)
        E=[jnp.where(inm,jnp.where(lane==8*p+k,1.0,0.0),rows[k]) for k in range(8)]
        m={}; rcp=[]; rs=[]
        for k in range(8):
            r=lax.rsqrt(B[k,k]); rs.append(r); rc=r*r; rcp.append(rc)
            for i in range(k+1,8):
                m[i,k]=B[k,i]*rc
            for i in range(k+1,8):
                for j in range(i,8):
                    B[i,j]=B[i,j]-m[i,k]*B[k,j]
                E[i]=E[i]-m[i,k]*E[k]
        V=[None]*8
        for k in reversed(range(8)):
            v=E[k]*rcp[k]
            for i in range(k+1,8):
                v=v-m[i,k]*V[i]
            V[k]=v
        o=E[7]*rs[7]
        for k in range(7):
            o=jnp.where(sub==k,E[k]*rs[k],o)
        out.append(jnp.where(lane<=8*p+sub,o,0.0))
        for q in range(p+1,n):
            c=[jnp.broadcast_to(tiles[q][:,8*p+k:8*p+k+1],(8,BLK)) for k in range(8)]
            t=jnp.where(inm,0.0,tiles[q])
            acc=[c[k]*V[k] for k in range(8)]
            while len(acc)>1:
                acc=[acc[i]+acc[i+1] for i in range(0,len(acc),2)]
            tiles[q]=t-acc[0]
    return out

def chol_body(g):
    def step(b,_):
        off=pl.multiple_of(b*BLK,BLK)
        tiles=[g[pl.ds(pl.multiple_of(off+8*t,8),8),pl.ds(off,BLK)] for t in range(16)]
        out=sweep(tiles)
        for t in range(16):
            g[pl.ds(pl.multiple_of(off+8*t,8),8),pl.ds(off,BLK)]=out[t]
        for bb in range(4):
            @pl.when(b==bb)
            def _():
                o=bb*BLK; e=o+BLK
                X=g[o:e,o:e]
                if bb>0: g[o:e,:o]=dot3(X,g[o:e,:o],NN)
                if bb<3:
                    L=dot3(g[e:,o:e],X,NT)
                    Yl=g[o:e,:e]
                    U=dot3(X,g[o:e,e:],NN)
                    if bb>0: g[e:,:o]=g[e:,:o]-dot3(L,Yl[:,:o],NN)
                    g[e:,o:e]=-dot3(L,X,NN)
                    g[e:,e:]=g[e:,e:]-dot3(L,U,NN)
        return 0
    lax.fori_loop(0,4,step,0)
    for bb in range(3):
        g[bb*BLK:(bb+1)*BLK,(bb+1)*BLK:]=jnp.zeros((BLK,NB-(bb+1)*BLK),F)


def factor_kernel(a_ref, l_ref, x_ref):
    x_ref[...] = a_ref[...]
    chol_body(x_ref)
    rb, cb = l_ref.shape
    ro = pl.multiple_of(lax.axis_index("row") * rb, rb)
    co = pl.multiple_of(lax.axis_index("col") * cb, cb)
    block = dot3(a_ref[pl.ds(ro, rb), :], x_ref[pl.ds(co, cb), :], NT)
    gi = ro + lax.broadcasted_iota(jnp.int32, (rb, cb), 0)
    gj = co + lax.broadcasted_iota(jnp.int32, (rb, cb), 1)
    l_ref[...] = jnp.where(gi >= gj, block, 0.0)


def factor_and_inverse(a, rb, cb):
    return pl.pallas_call(
        factor_kernel,
        out_shape=(jax.ShapeDtypeStruct((rb, cb), F), jax.ShapeDtypeStruct((NB, NB), F)),
        in_specs=[pl.BlockSpec(memory_space=pltpu.VMEM)],
        out_specs=[pl.BlockSpec(memory_space=pltpu.VMEM)] * 2,
        compiler_params=pltpu.CompilerParams(vmem_limit_bytes=40 << 20),
        cost_estimate=pl.CostEstimate(flops=4 * 10**9, bytes_accessed=3 << 20, transcendentals=0),
    )(a)


def split_dot(ah, al, bh, bl, dims):
    d = lambda x, y: lax.dot_general(x, y, (dims, ((), ())), preferred_element_type=F)
    return d(ah, bh) + (d(ah, bl) + d(al, bh))


def update_kernel(x_ref, pr_ref, pc_ref, slab_ref, out_ref, po_ref, xh, xl, ch, cl, tmp):
    i = pl.program_id(0)

    @pl.when(i == 0)
    def _():
        h, l = split(x_ref[...])
        xh[...] = h
        xl[...] = l
        ph, plo = split(pc_ref[...])
        f = split_dot(ph, plo, xh[...], xl[...], NT)
        h, l = split(f)
        ch[...] = h
        cl[...] = l

    ph, plo = split(pr_ref[...])
    f = split_dot(ph, plo, xh[...], xl[...], NT)
    tmp[...] = f
    h, l = split(f)
    out_ref[...] = slab_ref[...] - split_dot(h, l, ch[...], cl[...], NT)
    c = lax.axis_index("col")
    w = po_ref.shape[1]
    per = 128 // w
    chunk = tmp[:, pl.ds(pl.multiple_of((c // per) * 128, 128), 128)]
    shift = lax.rem(128 - (c % per) * w, 128)
    po_ref[...] = pltpu.roll(chunk, shift, 1)[:, :w]


def update(x, pr, pc, slab, w, tile=256):
    m, n = slab.shape
    full = lambda s: pl.BlockSpec(s, lambda i: (0, 0), pipeline_mode=pl.Buffered(1))
    rows = lambda k: pl.BlockSpec((tile, k), lambda i: (i, 0))
    return pl.pallas_call(
        update_kernel,
        grid=(m // tile,),
        out_shape=(jax.ShapeDtypeStruct((m, n), F), jax.ShapeDtypeStruct((m, w), F)),
        in_specs=[full((NB, NB)), rows(NB), full((n, NB)), rows(n)],
        out_specs=[rows(n), rows(w)],
        scratch_shapes=[pltpu.VMEM((NB, NB), jnp.bfloat16)] * 2
        + [pltpu.VMEM((n, NB), jnp.bfloat16)] * 2
        + [pltpu.VMEM((tile, NB), F)],
        compiler_params=pltpu.CompilerParams(vmem_limit_bytes=48 << 20),
    )(x, pr, pc, slab)


def body(diag_block, panel, slab):
    nr, nc = lax.axis_size("row"), lax.axis_size("col")
    block = lax.all_gather(diag_block, "row", axis=0, tiled=True)
    block = lax.all_gather(block, "col", axis=1, tiled=True)
    pr = lax.all_gather(panel, "col", axis=1, tiled=True)
    pairs = [(r * nc + c, c * nc + r) for r in range(nr) for c in range(nc)]
    turned = lax.ppermute(panel, ("row", "col"), pairs)
    pc = lax.all_gather(turned, "row", axis=1, tiled=True)
    factor_out, inverse = factor_and_inverse(block, *diag_block.shape)
    out, panel_out = update(inverse, pr, pc, slab, panel.shape[1])
    return factor_out, panel_out, out


def solution(mesh):
    spec = P("row", "col")
    return jax.shard_map(
        body, mesh=mesh, in_specs=(spec, spec, spec), out_specs=(spec, spec, spec), check_vma=False
    )
```

```python
import jax
import jax.numpy as jnp
from jax import lax
from jax.sharding import PartitionSpec as P
from jax.experimental import pallas as pl
from jax.experimental.pallas import tpu as pltpu
F=jnp.float32
NB=512; BLK=128

def split(x):
    hi=x.astype(jnp.bfloat16)
    lo=(x-hi.astype(F)).astype(jnp.bfloat16)
    return hi,lo
def dot3(a,b,dims):
    ah,al=split(a); bh,bl=split(b)
    d=lambda x,y: lax.dot_general(x,y,(dims,((),())),preferred_element_type=F)
    return d(ah,bh)+(d(ah,bl)+d(al,bh))
NN=((1,),(0,)); NT=((1,),(1,))

def sweep(tiles):
    lane=lax.broadcasted_iota(jnp.int32,(8,BLK),1)
    sub=lax.broadcasted_iota(jnp.int32,(8,BLK),0)
    n=len(tiles); out=[]
    tiles=list(tiles)
    for p in range(n):
        R=tiles[p]
        rows=[jnp.broadcast_to(R[k:k+1,:],(8,BLK)) for k in range(8)]
        B={(k,i):jnp.broadcast_to(rows[k][:,8*p+i:8*p+i+1],(8,BLK)) for k in range(8) for i in range(k,8)}
        inm=(lane>=8*p)&(lane<8*p+8)
        E=[jnp.where(inm,jnp.where(lane==8*p+k,1.0,0.0),rows[k]) for k in range(8)]
        m={}; rcp=[]; rs=[]
        for k in range(8):
            r=lax.rsqrt(B[k,k]); rs.append(r); rc=r*r; rcp.append(rc)
            for i in range(k+1,8):
                m[i,k]=B[k,i]*rc
            for i in range(k+1,8):
                for j in range(i,8):
                    B[i,j]=B[i,j]-m[i,k]*B[k,j]
                E[i]=E[i]-m[i,k]*E[k]
        V=[None]*8
        for k in reversed(range(8)):
            v=E[k]*rcp[k]
            for i in range(k+1,8):
                v=v-m[i,k]*V[i]
            V[k]=v
        o=E[7]*rs[7]
        for k in range(7):
            o=jnp.where(sub==k,E[k]*rs[k],o)
        out.append(jnp.where(lane<=8*p+sub,o,0.0))
        for q in range(p+1,n):
            c=[jnp.broadcast_to(tiles[q][:,8*p+k:8*p+k+1],(8,BLK)) for k in range(8)]
            t=jnp.where(inm,0.0,tiles[q])
            acc=[c[k]*V[k] for k in range(8)]
            while len(acc)>1:
                acc=[acc[i]+acc[i+1] for i in range(0,len(acc),2)]
            tiles[q]=t-acc[0]
    return out

def chol_body(g, hook):
    def step(b,_):
        off=pl.multiple_of(b*BLK,BLK)
        tiles=[g[pl.ds(pl.multiple_of(off+8*t,8),8),pl.ds(off,BLK)] for t in range(16)]
        out=sweep(tiles)
        for t in range(16):
            g[pl.ds(pl.multiple_of(off+8*t,8),8),pl.ds(off,BLK)]=out[t]
        for bb in range(4):
            @pl.when(b==bb)
            def _():
                o=bb*BLK; e=o+BLK
                X=g[o:e,o:e]
                if bb>0: g[o:e,:o]=dot3(X,g[o:e,:o],NN)
                if bb<3:
                    L=dot3(g[e:,o:e],X,NT)
                    Yl=g[o:e,:e]
                    U=dot3(X,g[o:e,e:],NN)
                    if bb>0: g[e:,:o]=g[e:,:o]-dot3(L,Yl[:,:o],NN)
                    g[e:,o:e]=-dot3(L,X,NN)
                    g[e:,e:]=g[e:,e:]-dot3(L,U,NN)
                hook(bb)
        return 0
    lax.fori_loop(0,4,step,0)
    for bb in range(3):
        g[bb*BLK:(bb+1)*BLK,(bb+1)*BLK:]=jnp.zeros((BLK,NB-(bb+1)*BLK),F)


MESH = pl.DeviceIdType.MESH


def factor_kernel(
    diag_ref, pt_ref, l_ref, x_ref, pr_ref, pc_ref, strip, a_ref,
    s1, r1, s2, r2, s3, r3, s4, r4, s5, r5, s6, r6, own,
):
    r = lax.axis_index("row")
    c = lax.axis_index("col")
    n = 16
    w = pt_ref.shape[0]
    core = lax.rem(r, 2)
    other = r + 1 - 2 * core
    at = lambda i: pl.ds(pl.multiple_of(i * w, w), w)

    barrier = pltpu.get_barrier_semaphore()

    def greet(t, _):
        pl.semaphore_signal(barrier, 1, device_id=(lax.rem(r + t, n), c), device_id_type=MESH)
        pl.semaphore_signal(barrier, 1, device_id=(r, lax.rem(c + t, n)), device_id_type=MESH)
        return 0

    lax.fori_loop(1, n, greet, 0)

    @pl.when(r != c)
    def _():
        pl.semaphore_signal(barrier, 1, device_id=(c, r), device_id_type=MESH)

    pl.semaphore_wait(barrier, 2 * (n - 1) + jnp.where(r == c, 0, 1))

    def diag_copy(src, peer):
        return pltpu.make_async_remote_copy(
            diag_ref, strip.at[at(src), :], s1.at[peer], r1.at[src], device_id=(peer, c), device_id_type=MESH)

    def strip_copy(src, peer):
        return pltpu.make_async_remote_copy(
            a_ref.at[at(src), :], a_ref.at[at(src), :], s2.at[peer], r2.at[src], device_id=(r, peer), device_id_type=MESH)

    def panel_copy(src, peer):
        return pltpu.make_async_remote_copy(
            pt_ref, pr_ref.at[at(src), :], s3.at[peer], r3.at[src], device_id=(r, peer), device_id_type=MESH)

    def turn_copy(src):
        return pltpu.make_async_remote_copy(
            pt_ref, pc_ref.at[at(src), :], s4, r4, device_id=(c, r), device_id_type=MESH)

    def z_copy(src, peer):
        row = 2 * src + core
        return pltpu.make_async_remote_copy(
            pc_ref.at[at(row), :], pc_ref.at[at(row), :], s5.at[peer], r5.at[src],
            device_id=(2 * peer + core, c), device_id_type=MESH)

    def twin_copy(z, side):
        row = 2 * z + side
        return pltpu.make_async_remote_copy(
            pc_ref.at[at(row), :], pc_ref.at[at(row), :], s6.at[z], r6.at[z],
            device_id=(other, c), device_id_type=MESH)

    def each(count, me, fn):
        def step(t, _):
            fn(lax.rem(me + t, count))
            return 0
        lax.fori_loop(1, count, step, 0)

    each(n, r, lambda p: diag_copy(r, p).start())

    @pl.when(r != c)
    def _():
        turn_copy(c).start()

    @pl.when(r == c)
    def _():
        cp = pltpu.make_async_copy(pt_ref, pc_ref.at[at(r), :], r4)
        cp.start()

    mine = pltpu.make_async_copy(pt_ref, pr_ref.at[at(c), :], own)
    mine.start()
    strip[at(r), :] = diag_ref[...]
    each(n, r, lambda p: diag_copy(p, p).wait_recv())
    a_ref[at(c), :] = strip[...].T
    each(n, c, lambda p: strip_copy(c, p).start())
    each(n, c, lambda p: panel_copy(c, p).start())

    z = r // 2

    @pl.when(r != c)
    def _():
        turn_copy(r).wait_recv()

    @pl.when(r == c)
    def _():
        pltpu.make_async_copy(pt_ref, pc_ref.at[at(r), :], r4).wait()

    each(n // 2, z, lambda p: z_copy(z, p).start())
    each(n, c, lambda p: strip_copy(p, p).wait_recv())
    x_ref[...] = a_ref[...]

    def hook(b):
        if b == 2:
            twin_copy(z, core).start()

            def forward(p):
                z_copy(p, p).wait_recv()
                twin_copy(p, core).start()

            each(n // 2, z, forward)

    chol_body(x_ref, hook)

    rb, cb = l_ref.shape
    block = dot3(a_ref[at(r), :], x_ref[at(c), :], NT)
    gi = r * rb + lax.broadcasted_iota(jnp.int32, (rb, cb), 0)
    gj = c * cb + lax.broadcasted_iota(jnp.int32, (rb, cb), 1)
    l_ref[...] = jnp.where(gi >= gj, block, 0.0)

    each(n, r, lambda p: diag_copy(r, p).wait_send())
    each(n, c, lambda p: strip_copy(c, p).wait_send())
    each(n, c, lambda p: panel_copy(c, p).wait_send())
    each(n, c, lambda p: panel_copy(p, p).wait_recv())
    mine.wait()

    @pl.when(r != c)
    def _():
        turn_copy(c).wait_send()

    each(n // 2, z, lambda p: z_copy(z, p).wait_send())

    def last(t, _):
        twin_copy(t, core).wait_send()
        twin_copy(t, 1 - core).wait_recv()
        return 0

    lax.fori_loop(0, n // 2, last, 0)


def factor_and_gather(diag, pt):
    w, m = pt.shape
    dma = pltpu.SemaphoreType.DMA
    any_space = pl.BlockSpec(memory_space=pl.ANY)
    vmem = pl.BlockSpec(memory_space=pltpu.VMEM)
    return pl.pallas_call(
        factor_kernel,
        out_shape=(
            jax.ShapeDtypeStruct(diag.shape, F),
            jax.ShapeDtypeStruct((NB, NB), F),
            jax.ShapeDtypeStruct((NB, m), F),
            jax.ShapeDtypeStruct((NB, m), F),
        ),
        in_specs=[vmem, any_space],
        out_specs=[vmem, vmem, any_space, any_space],
        scratch_shapes=[pltpu.VMEM((NB, w), F), pltpu.VMEM((NB, NB), F)]
        + [dma((16,))] * 6 + [dma(()), dma(())] + [dma((8,))] * 4 + [dma(())],
        compiler_params=pltpu.CompilerParams(
            vmem_limit_bytes=40 << 20, collective_id=0, has_side_effects=True),
    )(diag, pt)


def split_dot(ah, al, bh, bl, dims):
    d = lambda x, y: lax.dot_general(x, y, (dims, ((), ())), preferred_element_type=F)
    return d(ah, bh) + (d(ah, bl) + d(al, bh))


def update_kernel(x_ref, pr_ref, pc_ref, slab_ref, out_ref, po_ref, xh, xl, ch, cl, tmp):
    i = pl.program_id(0)

    @pl.when(i == 0)
    def _():
        h, l = split(x_ref[...])
        xh[...] = h
        xl[...] = l
        ph, plo = split(pc_ref[...])
        f = split_dot(xh[...], xl[...], ph, plo, NN)
        h, l = split(f)
        ch[...] = h
        cl[...] = l

    ph, plo = split(pr_ref[...])
    f = split_dot(xh[...], xl[...], ph, plo, NN)
    tmp[...] = f
    h, l = split(f.T)
    out_ref[...] = slab_ref[...] - split_dot(h, l, ch[...], cl[...], NN)
    w = po_ref.shape[0]
    po_ref[...] = tmp[pl.ds(pl.multiple_of(lax.axis_index("col") * w, w), w), :]


def update(x, pr, pc, slab, w, tile=256):
    m, n = slab.shape
    full = lambda s: pl.BlockSpec(s, lambda i: (0, 0), pipeline_mode=pl.Buffered(1))
    rows = lambda k: pl.BlockSpec((tile, k), lambda i: (i, 0))
    cols = lambda k: pl.BlockSpec((k, tile), lambda i: (0, i))
    return pl.pallas_call(
        update_kernel,
        grid=(m // tile,),
        out_shape=(jax.ShapeDtypeStruct((m, n), F), jax.ShapeDtypeStruct((w, m), F)),
        in_specs=[full((NB, NB)), cols(NB), full((NB, n)), rows(n)],
        out_specs=[rows(n), cols(w)],
        scratch_shapes=[pltpu.VMEM((NB, NB), jnp.bfloat16)] * 2
        + [pltpu.VMEM((NB, n), jnp.bfloat16)] * 2
        + [pltpu.VMEM((NB, tile), F)],
        compiler_params=pltpu.CompilerParams(vmem_limit_bytes=48 << 20),
    )(x, pr, pc, slab)


def body(diag_block, panel, slab):
    factor_out, inverse, pr, pc = factor_and_gather(diag_block, panel.T)
    out, panel_out = update(inverse, pr, pc, slab, panel.shape[1])
    return factor_out, panel_out.T, out


def solution(mesh):
    spec = P("row", "col")
    return jax.shard_map(
        body, mesh=mesh, in_specs=(spec, spec, spec), out_specs=(spec, spec, spec), check_vma=False
    )
```

```python
import jax
import jax.numpy as jnp
from jax import lax
from jax.sharding import PartitionSpec as P
from jax.experimental import pallas as pl
from jax.experimental.pallas import tpu as pltpu
F=jnp.float32
NB=512; BLK=128

def split(x):
    hi=x.astype(jnp.bfloat16)
    lo=(x-hi.astype(F)).astype(jnp.bfloat16)
    return hi,lo
def dot3(a,b,dims):
    ah,al=split(a); bh,bl=split(b)
    d=lambda x,y: lax.dot_general(x,y,(dims,((),())),preferred_element_type=F)
    return d(ah,bh)+(d(ah,bl)+d(al,bh))
NN=((1,),(0,)); NT=((1,),(1,))

def sweep(tiles):
    lane=lax.broadcasted_iota(jnp.int32,(8,BLK),1)
    sub=lax.broadcasted_iota(jnp.int32,(8,BLK),0)
    n=len(tiles); out=[]
    tiles=list(tiles)
    for p in range(n):
        R=tiles[p]
        rows=[jnp.broadcast_to(R[k:k+1,:],(8,BLK)) for k in range(8)]
        B={(k,i):jnp.broadcast_to(rows[k][:,8*p+i:8*p+i+1],(8,BLK)) for k in range(8) for i in range(k,8)}
        inm=(lane>=8*p)&(lane<8*p+8)
        E=[jnp.where(inm,jnp.where(lane==8*p+k,1.0,0.0),rows[k]) for k in range(8)]
        m={}; rcp=[]; rs=[]
        for k in range(8):
            r=lax.rsqrt(B[k,k]); rs.append(r); rc=r*r; rcp.append(rc)
            for i in range(k+1,8):
                m[i,k]=B[k,i]*rc
            for i in range(k+1,8):
                for j in range(i,8):
                    B[i,j]=B[i,j]-m[i,k]*B[k,j]
                E[i]=E[i]-m[i,k]*E[k]
        V=[None]*8
        for k in reversed(range(8)):
            v=E[k]*rcp[k]
            for i in range(k+1,8):
                v=v-m[i,k]*V[i]
            V[k]=v
        o=E[7]*rs[7]
        for k in range(7):
            o=jnp.where(sub==k,E[k]*rs[k],o)
        out.append(jnp.where(lane<=8*p+sub,o,0.0))
        for q in range(p+1,n):
            c=[jnp.broadcast_to(tiles[q][:,8*p+k:8*p+k+1],(8,BLK)) for k in range(8)]
            t=jnp.where(inm,0.0,tiles[q])
            acc=[c[k]*V[k] for k in range(8)]
            while len(acc)>1:
                acc=[acc[i]+acc[i+1] for i in range(0,len(acc),2)]
            tiles[q]=t-acc[0]
    return out


MESH = pl.DeviceIdType.MESH


def factor_blocks(a, u, x, s, arrive, hook):
    def step(b, _):
        for bb in range(4):
            o, e = bb * BLK, (bb + 1) * BLK

            @pl.when(b == bb)
            def _():
                arrive(bb)
                if bb == 0:
                    s[...] = a[0:BLK, :]
                else:
                    wt = u[0:o, o:e].T
                    s[:, :o] = -dot3(wt, x[0:o, 0:o], NN)
                    s[:, o:] = a[o:e, o:] - dot3(wt, u[0:o, o:], NN)

        off = pl.multiple_of(b * BLK, BLK)
        out = sweep([s[8 * t : 8 * t + 8, pl.ds(off, BLK)] for t in range(16)])
        for t in range(16):
            x[pl.ds(pl.multiple_of(off + 8 * t, 8), 8), pl.ds(off, BLK)] = out[t]
        for bb in range(4):
            o, e = bb * BLK, (bb + 1) * BLK

            @pl.when(b == bb)
            def _():
                inv = x[o:e, o:e]
                u[o:e, o:] = dot3(inv, s[:, o:], NN)
                if bb > 0:
                    x[o:e, :o] = dot3(inv, s[:, :o], NN)
                if bb < 3:
                    x[o:e, e:] = jnp.zeros((BLK, NB - e), F)
                hook(bb)

        return 0

    lax.fori_loop(0, 4, step, 0)


def factor_kernel(
    diag_ref, pt_ref, l_ref, x_ref, pr_ref, pc_ref, pack, strip, tb, a_ref, u_ref, s_ref,
    s1, r1, s2, r2, sx, rx, sy, ry, sx2, rx2, sy2, ry2, st, s5, r5, s6, r6, own,
):
    r = lax.axis_index("row")
    c = lax.axis_index("col")
    n = 16
    w, m = pt_ref.shape
    z = r // 2
    core = lax.rem(r, 2)
    away = lax.rem(r - c + n, n)
    other = r + 1 - 2 * core
    cy, cx = c // 4, lax.rem(c, 4)
    at = lambda i: pl.ds(pl.multiple_of(i * w, w), w)
    at4 = lambda i: pl.ds(pl.multiple_of(i * 4 * w, 4 * w), 4 * w)
    left, right = pl.ds(0, m // 2), pl.ds(m // 2, m // 2)

    def loop(start, stop, fn):
        def step(t, _):
            fn(t)
            return 0

        lax.fori_loop(start, stop, step, 0)

    def each(count, me, fn):
        loop(1, count, lambda t: fn(lax.rem(me + t, count)))

    barrier = pltpu.get_barrier_semaphore()

    def greet(row, col):
        pl.semaphore_signal(barrier, 1, device_id=(row, col), device_id_type=MESH)

    each(n, r, lambda p: greet(p, c))
    each(n, c, lambda p: greet(r, p))
    pl.semaphore_wait(barrier, 2 * (n - 1))

    def remote(src, dst, send, recv, row, col):
        return pltpu.make_async_remote_copy(src, dst, send, recv, device_id=(row, col), device_id_type=MESH)

    pw = pack.shape[0] // n
    at8 = lambda i: pl.ds(pl.multiple_of(i * pw, pw), pw)

    def diag_copy(src, peer):
        part = pack.at[at8(src), :]
        return remote(part, part, s1.at[peer], r1.at[src], peer, c)

    def strip_copy(src, peer, q):
        part = a_ref.at[at(src), q * BLK :]
        return remote(part, part, s2.at[peer], r2.at[src], r, peer)

    def x_first(src, peer):
        return remote(pt_ref.at[:, left], pr_ref.at[at(4 * cy + src), left], sx.at[peer], rx.at[src], r, 4 * cy + peer)

    def y_first(src, peer):
        return remote(pt_ref.at[:, right], pr_ref.at[at(4 * src + cx), right], sy.at[peer], ry.at[src], r, 4 * peer + cx)

    def y_second(src, peer):
        part = pr_ref.at[at4(src), left]
        return remote(part, part, sy2.at[peer], ry2.at[src], r, 4 * peer + cx)

    def x_second(src, peer, j):
        part = pr_ref.at[at(4 * j + src), right]
        return remote(part, part, sx2.at[4 * peer + j], rx2.at[4 * src + j], r, 4 * cy + peer)

    def turn_z():
        return remote(pt_ref, tb, st.at[0], st.at[1], lax.rem(r + c, n), c)

    def turn_plane():
        return remote(tb, pc_ref.at[at(c), :], st.at[2], st.at[3], r, away)

    def turn_plane_in():
        return remote(tb, pc_ref.at[at(away), :], st.at[2], st.at[3], r, away)

    def turn_local(src, dst):
        return pltpu.make_async_copy(src, dst, own.at[1])

    def z_row(t):
        return 2 * lax.rem(z + t + 8, 8) + core

    def piece(t, side):
        return pc_ref.at[at(lax.rem(2 * lax.rem(z + t + 8, 8) + side - c + n, n)), :]

    def z_copy(i, src, to):
        part = piece(src, core)
        return remote(part, part, s5.at[i], r5.at[(src - to) % 8], z_row(to), c)

    def z_in(src):
        part = piece(src, core)
        return remote(part, part, s5.at[0], r5.at[src % 8], r, c)

    def twin_copy(t, side):
        part = piece(t, side)
        return remote(part, part, s6.at[t % 8], r6.at[t % 8], other, c)

    first = ((0, 2), (0, -2), (0, 1), (0, -1))
    relay = ((-2, 2), (-2, 1), (2, -1))

    block = diag_ref[...]
    pack[at8(r), :] = jnp.concatenate([block[pw * j : pw * j + pw, :] for j in range(w // pw)], axis=1)
    each(n, r, lambda p: diag_copy(r, p).start())
    keep = pltpu.make_async_copy(pt_ref, pr_ref.at[at(c), :], own.at[0])
    keep.start()
    each(4, cx, lambda p: x_first(cx, p).start())
    each(4, cy, lambda p: y_first(cy, p).start())

    @pl.when(c != 0)
    def _():
        turn_z().start()

    @pl.when(c == 0)
    def _():
        turn_local(pt_ref, tb).start()

    each(n, r, lambda p: diag_copy(p, p).wait_recv())
    for i in range(n):
        packed = pack[pw * i : pw * i + pw, :]
        for j in range(w // pw):
            moved = packed if j == 0 else pltpu.roll(packed, BLK - w * j, 1)
            strip[w * i + pw * j : w * i + pw * j + pw, :] = moved[:, :w]
    a_ref[at(c), :] = strip[...].T
    group = c // 4

    def strips(fn):
        for q in range(4):

            @pl.when(group == q)
            def _():
                each(n, c, lambda p: fn(p, q))

    strips(lambda p, q: strip_copy(c, p, q).start())

    @pl.when(c != 0)
    def _():
        turn_z().wait()

    @pl.when(c == 0)
    def _():
        turn_local(pt_ref, tb).wait()

    @pl.when(away != c)
    def _():
        turn_plane().start()

    @pl.when(away == c)
    def _():
        turn_local(tb, pc_ref.at[at(c), :]).start()

    def arrive(bb):
        def one(t):
            @pl.when(t != c)
            def _():
                strip_copy(t, t, bb).wait_recv()

        loop(4 * bb, 4 * bb + 4, one)
        if bb == 0:

            @pl.when(away != c)
            def _():
                turn_plane_in().wait()

            @pl.when(away == c)
            def _():
                turn_local(tb, pc_ref.at[at(c), :]).wait()

            for i, (src, to) in enumerate(first):
                z_copy(i, src, to).start()
            keep.wait()
            each(4, cx, lambda p: x_first(p, p).wait_recv())
            each(4, cy, lambda p: y_second(cy, p).start())
            each(4, cy, lambda p: y_first(p, p).wait_recv())
            for j in range(4):
                each(4, cx, lambda p: x_second(cx, p, j).start())

    def hook(bb):
        if bb == 0:
            z_in(-2).wait_recv()
            z_in(2).wait_recv()
            for i, (src, to) in enumerate(relay):
                z_copy(4 + i, src, to).start()
            for t in (0, 2, -2):
                twin_copy(t, core).start()
        if bb == 2:
            for t in (1, -1, 3, -3, 4):
                z_in(t).wait_recv()
                twin_copy(t, core).start()

    factor_blocks(a_ref, u_ref, x_ref, s_ref, arrive, hook)

    rows, cols = l_ref.shape
    per = BLK // w
    chunk = u_ref[at(c), pl.ds(pl.multiple_of((r // per) * BLK, BLK), BLK)]
    turned = pltpu.roll(chunk, lax.rem(BLK - lax.rem(r, per) * w, BLK), 1)[:, :w].T
    gi = r * w + lax.broadcasted_iota(jnp.int32, (rows, cols), 0)
    gj = c * w + lax.broadcasted_iota(jnp.int32, (rows, cols), 1)
    l_ref[...] = jnp.where(gi >= gj, turned, 0.0)

    each(n, r, lambda p: diag_copy(r, p).wait_send())
    strips(lambda p, q: strip_copy(c, p, q).wait_send())
    each(4, cx, lambda p: x_first(cx, p).wait_send())
    each(4, cy, lambda p: y_first(cy, p).wait_send())
    for i, (src, to) in enumerate(first + relay):
        z_copy(i, src, to).wait_send()
    each(4, cy, lambda p: y_second(cy, p).wait_send())
    each(4, cy, lambda p: y_second(p, p).wait_recv())
    for j in range(4):
        each(4, cx, lambda p: x_second(cx, p, j).wait_send())
        each(4, cx, lambda p: x_second(p, p, j).wait_recv())

    for t in range(8):
        twin_copy(t, core).wait_send()
        twin_copy(t, 1 - core).wait_recv()


def factor_and_gather(diag, pt):
    w, m = pt.shape
    dma = pltpu.SemaphoreType.DMA
    any_space = pl.BlockSpec(memory_space=pl.ANY)
    vmem = pl.BlockSpec(memory_space=pltpu.VMEM)
    return pl.pallas_call(
        factor_kernel,
        out_shape=(
            jax.ShapeDtypeStruct(diag.shape, F),
            jax.ShapeDtypeStruct((NB, NB), F),
            jax.ShapeDtypeStruct((NB, m), F),
            jax.ShapeDtypeStruct((NB, m), F),
        ),
        in_specs=[vmem, any_space],
        out_specs=[vmem, vmem, any_space, any_space],
        scratch_shapes=[
            pltpu.VMEM((w * NB // BLK, BLK), F),
            pltpu.VMEM((NB, w), F),
            pltpu.VMEM((w, m), F),
            pltpu.VMEM((NB, NB), F),
            pltpu.VMEM((NB, NB), F),
            pltpu.VMEM((BLK, NB), F),
        ]
        + [dma((16,))] * 4
        + [dma((4,))] * 4
        + [dma((16,)), dma((16,)), dma((4,)), dma((4,))]
        + [dma((4,)), dma((8,)), dma((8,)), dma((8,)), dma((8,)), dma((2,))],
        compiler_params=pltpu.CompilerParams(
            vmem_limit_bytes=40 << 20, collective_id=0, has_side_effects=True
        ),
    )(diag, pt)


def split_dot(ah, al, bh, bl, dims):
    d = lambda x, y: lax.dot_general(x, y, (dims, ((), ())), preferred_element_type=F)
    return d(ah, bh) + (d(ah, bl) + d(al, bh))


def update_kernel(x_ref, pr_ref, pc_ref, slab_ref, out_ref, po_ref, xh, xl, ch, cl, tmp):
    i = pl.program_id(0)

    @pl.when(i == 0)
    def _():
        h, l = split(x_ref[...])
        xh[...] = h
        xl[...] = l
        ph, plo = split(pc_ref[...])
        f = split_dot(xh[...], xl[...], ph, plo, NN)
        h, l = split(f)
        ch[...] = h
        cl[...] = l

    ph, plo = split(pr_ref[...])
    f = split_dot(xh[...], xl[...], ph, plo, NN)
    tmp[...] = f
    h, l = split(f.T)
    out_ref[...] = slab_ref[...] - split_dot(h, l, ch[...], cl[...], NN)
    w = po_ref.shape[0]
    po_ref[...] = tmp[pl.ds(pl.multiple_of(lax.axis_index("col") * w, w), w), :]


def update(x, pr, pc, slab, w, tile=256):
    m, n = slab.shape
    full = lambda s: pl.BlockSpec(s, lambda i: (0, 0), pipeline_mode=pl.Buffered(1))
    rows = lambda k: pl.BlockSpec((tile, k), lambda i: (i, 0))
    cols = lambda k: pl.BlockSpec((k, tile), lambda i: (0, i))
    return pl.pallas_call(
        update_kernel,
        grid=(m // tile,),
        out_shape=(jax.ShapeDtypeStruct((m, n), F), jax.ShapeDtypeStruct((w, m), F)),
        in_specs=[full((NB, NB)), cols(NB), full((NB, n)), rows(n)],
        out_specs=[rows(n), cols(w)],
        scratch_shapes=[pltpu.VMEM((NB, NB), jnp.bfloat16)] * 2
        + [pltpu.VMEM((NB, n), jnp.bfloat16)] * 2
        + [pltpu.VMEM((NB, tile), F)],
        compiler_params=pltpu.CompilerParams(vmem_limit_bytes=48 << 20),
    )(x, pr, pc, slab)


def body(diag_block, panel, slab):
    factor_out, inverse, pr, pc = factor_and_gather(diag_block, panel.T)
    out, panel_out = update(inverse, pr, pc, slab, panel.shape[1])
    return factor_out, panel_out.T, out


def solution(mesh):
    spec = P("row", "col")
    return jax.shard_map(
        body, mesh=mesh, in_specs=(spec, spec, spec), out_specs=(spec, spec, spec), check_vma=False
    )
```

```python
import jax
import jax.numpy as jnp
from jax import lax
from jax.sharding import PartitionSpec as P
from jax.experimental import pallas as pl
from jax.experimental.pallas import tpu as pltpu
F=jnp.float32
NB=512; BLK=128

def split(x):
    hi=x.astype(jnp.bfloat16)
    lo=(x-hi.astype(F)).astype(jnp.bfloat16)
    return hi,lo
def dot3(a,b,dims):
    ah,al=split(a); bh,bl=split(b)
    d=lambda x,y: lax.dot_general(x,y,(dims,((),())),preferred_element_type=F)
    return d(ah,bh)+(d(ah,bl)+d(al,bh))
NN=((1,),(0,)); NT=((1,),(1,))

def sweep(tiles):
    lane=lax.broadcasted_iota(jnp.int32,(8,BLK),1)
    sub=lax.broadcasted_iota(jnp.int32,(8,BLK),0)
    n=len(tiles); out=[]
    tiles=list(tiles)
    for p in range(n):
        R=tiles[p]
        rows=[jnp.broadcast_to(R[k:k+1,:],(8,BLK)) for k in range(8)]
        C=[jnp.broadcast_to(R[:,8*p+i:8*p+i+1],(8,BLK)) for i in range(8)]
        B={(k,i):jnp.broadcast_to(C[k][i:i+1,:],(8,BLK)) for k in range(8) for i in range(k,8)}
        inm=(lane>=8*p)&(lane<8*p+8)
        E=[jnp.where(inm,jnp.where(lane==8*p+k,1.0,0.0),rows[k]) for k in range(8)]
        m={}; rcp=[]; rs=[]
        nxt=None
        if p+1<n:
            nc=[jnp.broadcast_to(tiles[p+1][:,8*p+k:8*p+k+1],(8,BLK)) for k in range(8)]
            nxt=jnp.where(inm,0.0,tiles[p+1])
        for k in range(8):
            rc=1.0/B[k,k]; rs.append(lax.rsqrt(B[k,k])); rcp.append(rc)
            for i in range(k+1,8):
                m[i,k]=B[k,i]*rc
            for i in range(k+1,8):
                for j in range(i,8):
                    B[i,j]=B[i,j]-m[i,k]*B[k,j]
                E[i]=E[i]-m[i,k]*E[k]
            if nxt is not None:
                for i in range(k+1,8):
                    nc[i]=nc[i]-m[i,k]*nc[k]
                nxt=nxt-(nc[k]*rc)*E[k]
        V=[None]*8
        for k in reversed(range(8)):
            v=E[k]*rcp[k]
            for i in range(k+1,8):
                v=v-m[i,k]*V[i]
            V[k]=v
        o=E[7]*rs[7]
        for k in range(7):
            o=jnp.where(sub==k,E[k]*rs[k],o)
        out.append(jnp.where(lane<=8*p+sub,o,0.0))
        if nxt is not None: tiles[p+1]=nxt
        for q in range(p+2,n):
            c=[jnp.broadcast_to(tiles[q][:,8*p+k:8*p+k+1],(8,BLK)) for k in range(8)]
            t=jnp.where(inm,0.0,tiles[q])
            acc=[c[k]*V[k] for k in range(8)]
            while len(acc)>1:
                acc=[acc[i]+acc[i+1] for i in range(0,len(acc),2)]
            tiles[q]=t-acc[0]
    return out


MESH = pl.DeviceIdType.MESH


def factor_blocks(a, u, x, s, arrive, rest, hook):
    def step(b, _):
        for bb in range(4):
            o, e = bb * BLK, (bb + 1) * BLK

            @pl.when(b == bb)
            def _():
                arrive(bb)
                if bb == 0:
                    s[:, 0:BLK] = a[0:BLK, 0:BLK]
                else:
                    wt = u[0:o, o:e].T
                    s[:, :o] = -dot3(wt, x[0:o, 0:o], NN)
                    s[:, o:] = a[o:e, o:] - dot3(wt, u[0:o, o:], NN)

        off = pl.multiple_of(b * BLK, BLK)
        out = sweep([s[8 * t : 8 * t + 8, pl.ds(off, BLK)] for t in range(16)])
        for t in range(16):
            x[pl.ds(pl.multiple_of(off + 8 * t, 8), 8), pl.ds(off, BLK)] = out[t]
        for bb in range(4):
            o, e = bb * BLK, (bb + 1) * BLK

            @pl.when(b == bb)
            def _():
                inv = x[o:e, o:e]
                if bb == 0:
                    rest()
                    s[:, BLK:] = a[0:BLK, BLK:]
                u[o:e, o:] = dot3(inv, s[:, o:], NN)
                if bb > 0:
                    x[o:e, :o] = dot3(inv, s[:, :o], NN)
                if bb < 3:
                    x[o:e, e:] = jnp.zeros((BLK, NB - e), F)
                hook(bb)

        return 0

    lax.fori_loop(0, 4, step, 0)


def factor_kernel(
    diag_in, pt_in, l_ref, x_ref, pr_ref, pc_ref, diag_ref, pt_ref, pack, strip, tb, a_ref, u_ref, s_ref,
    s1, r1, s2, r2, s2b, r2b, sx, rx, sy, ry, sx2, rx2, sy2, ry2, st, s5, r5, s6, r6, own,
):
    r = lax.axis_index("row")
    c = lax.axis_index("col")
    n = 16
    w, m = pt_ref.shape
    z = r // 2
    core = lax.rem(r, 2)
    away = lax.rem(r - c + n, n)
    other = r + 1 - 2 * core
    cy, cx = c // 4, lax.rem(c, 4)
    at = lambda i: pl.ds(pl.multiple_of(i * w, w), w)
    at4 = lambda i: pl.ds(pl.multiple_of(i * 4 * w, 4 * w), 4 * w)
    left, right = pl.ds(0, m // 2), pl.ds(m // 2, m // 2)

    def loop(start, stop, fn):
        def step(t, _):
            fn(t)
            return 0

        lax.fori_loop(start, stop, step, 0)

    def each(count, me, fn):
        loop(1, count, lambda t: fn(lax.rem(me + t, count)))

    fetch = [
        pltpu.make_async_copy(diag_in, diag_ref, own.at[0]),
        pltpu.make_async_copy(pt_in, pt_ref, own.at[1]),
    ]
    for copy in fetch:
        copy.start()
    barrier = pltpu.get_barrier_semaphore()

    def greet(row, col):
        pl.semaphore_signal(barrier, 1, device_id=(row, col), device_id_type=MESH)

    each(n, r, lambda p: greet(p, c))
    each(n, c, lambda p: greet(r, p))
    pl.semaphore_wait(barrier, 2 * (n - 1))

    def remote(src, dst, send, recv, row, col):
        return pltpu.make_async_remote_copy(src, dst, send, recv, device_id=(row, col), device_id_type=MESH)

    pw = pack.shape[0] // n
    at8 = lambda i: pl.ds(pl.multiple_of(i * pw, pw), pw)

    def diag_copy(src, peer):
        part = pack.at[at8(src), :]
        return remote(part, part, s1.at[peer], r1.at[src], peer, c)

    def strip_copy(src, peer, q):
        part = a_ref.at[at(src), q * BLK :] if q else a_ref.at[at(src), 0:BLK]
        return remote(part, part, s2.at[peer], r2.at[src], r, peer)

    def rest_copy(src, peer):
        part = a_ref.at[at(src), BLK:]
        return remote(part, part, s2b.at[peer], r2b.at[src], r, peer)

    def x_first(src, peer):
        return remote(pt_ref.at[:, left], pr_ref.at[at(4 * cy + src), left], sx.at[peer], rx.at[src], r, 4 * cy + peer)

    def y_first(src, peer):
        return remote(pt_ref.at[:, right], pr_ref.at[at(4 * src + cx), right], sy.at[peer], ry.at[src], r, 4 * peer + cx)

    def y_second(src, peer):
        part = pr_ref.at[at4(src), left]
        return remote(part, part, sy2.at[peer], ry2.at[src], r, 4 * peer + cx)

    def x_second(src, peer, j):
        part = pr_ref.at[at(4 * j + src), right]
        return remote(part, part, sx2.at[4 * peer + j], rx2.at[4 * src + j], r, 4 * cy + peer)

    def turn_z():
        return remote(pt_ref, tb, st.at[0], st.at[1], lax.rem(r + c, n), c)

    def turn_plane():
        return remote(tb, pc_ref.at[at(c), :], st.at[2], st.at[3], r, away)

    def turn_plane_in():
        return remote(tb, pc_ref.at[at(away), :], st.at[2], st.at[3], r, away)

    def turn_local(src, dst):
        return pltpu.make_async_copy(src, dst, own.at[1])

    def z_row(t):
        return 2 * lax.rem(z + t + 8, 8) + core

    def piece(t, side):
        return pc_ref.at[at(lax.rem(2 * lax.rem(z + t + 8, 8) + side - c + n, n)), :]

    def z_copy(i, src, to):
        part = piece(src, core)
        return remote(part, part, s5.at[i], r5.at[(src - to) % 8], z_row(to), c)

    def z_in(src):
        part = piece(src, core)
        return remote(part, part, s5.at[0], r5.at[src % 8], r, c)

    def twin_copy(t, side):
        part = piece(t, side)
        return remote(part, part, s6.at[t % 8], r6.at[t % 8], other, c)

    first = ((0, 2), (0, -2), (0, 1), (0, -1))
    relay = ((-2, 2), (-2, 1), (2, -1))

    fetch[0].wait()
    block = diag_ref[...]
    pack[at8(r), :] = jnp.concatenate([block[pw * j : pw * j + pw, :] for j in range(w // pw)], axis=1)
    each(n, r, lambda p: diag_copy(r, p).start())
    fetch[1].wait()
    keep = pltpu.make_async_copy(pt_ref, pr_ref.at[at(c), :], own.at[0])
    keep.start()
    each(4, cx, lambda p: x_first(cx, p).start())
    each(4, cy, lambda p: y_first(cy, p).start())

    @pl.when(c != 0)
    def _():
        turn_z().start()

    @pl.when(c == 0)
    def _():
        turn_local(pt_ref, tb).start()

    each(n, r, lambda p: diag_copy(p, p).wait_recv())
    for i in range(n):
        packed = pack[pw * i : pw * i + pw, :]
        for j in range(w // pw):
            moved = packed if j == 0 else pltpu.roll(packed, BLK - w * j, 1)
            strip[w * i + pw * j : w * i + pw * j + pw, :] = moved[:, :w]
    a_ref[at(c), :] = strip[...].T
    group = c // 4

    def strips(fn, more):
        for q in range(4):

            @pl.when(group == q)
            def _():
                each(n, c, lambda p: fn(p, q))
                if q == 0:
                    each(n, c, more)

    strips(lambda p, q: strip_copy(c, p, q).start(), lambda p: rest_copy(c, p).start())

    @pl.when(c != 0)
    def _():
        turn_z().wait()

    @pl.when(c == 0)
    def _():
        turn_local(pt_ref, tb).wait()

    @pl.when(away != c)
    def _():
        turn_plane().start()

    @pl.when(away == c)
    def _():
        turn_local(tb, pc_ref.at[at(c), :]).start()

    def arrive(bb):
        def one(t):
            @pl.when(t != c)
            def _():
                strip_copy(t, t, bb).wait_recv()

        loop(4 * bb, 4 * bb + 4, one)
        if bb == 0:

            @pl.when(away != c)
            def _():
                turn_plane_in().wait()

            @pl.when(away == c)
            def _():
                turn_local(tb, pc_ref.at[at(c), :]).wait()

            for i, (src, to) in enumerate(first):
                z_copy(i, src, to).start()
            keep.wait()
            each(4, cx, lambda p: x_first(p, p).wait_recv())
            each(4, cy, lambda p: y_second(cy, p).start())
            each(4, cy, lambda p: y_first(p, p).wait_recv())
            for j in range(4):
                each(4, cx, lambda p: x_second(cx, p, j).start())

    def rest():
        def one(t):
            @pl.when(t != c)
            def _():
                rest_copy(t, t).wait_recv()

        loop(0, 4, one)

    def hook(bb):
        if bb == 0:
            z_in(-2).wait_recv()
            z_in(2).wait_recv()
            for i, (src, to) in enumerate(relay):
                z_copy(4 + i, src, to).start()
            for t in (0, 2, -2):
                twin_copy(t, core).start()
        if bb == 2:
            for t in (1, -1, 3, -3, 4):
                z_in(t).wait_recv()
                twin_copy(t, core).start()

    factor_blocks(a_ref, u_ref, x_ref, s_ref, arrive, rest, hook)

    rows, cols = l_ref.shape
    per = BLK // w
    chunk = u_ref[at(c), pl.ds(pl.multiple_of((r // per) * BLK, BLK), BLK)]
    turned = pltpu.roll(chunk, lax.rem(BLK - lax.rem(r, per) * w, BLK), 1)[:, :w].T
    gi = r * w + lax.broadcasted_iota(jnp.int32, (rows, cols), 0)
    gj = c * w + lax.broadcasted_iota(jnp.int32, (rows, cols), 1)
    l_ref[...] = jnp.where(gi >= gj, turned, 0.0)

    each(n, r, lambda p: diag_copy(r, p).wait_send())
    strips(lambda p, q: strip_copy(c, p, q).wait_send(), lambda p: rest_copy(c, p).wait_send())
    each(4, cx, lambda p: x_first(cx, p).wait_send())
    each(4, cy, lambda p: y_first(cy, p).wait_send())
    for i, (src, to) in enumerate(first + relay):
        z_copy(i, src, to).wait_send()
    each(4, cy, lambda p: y_second(cy, p).wait_send())
    each(4, cy, lambda p: y_second(p, p).wait_recv())
    for j in range(4):
        each(4, cx, lambda p: x_second(cx, p, j).wait_send())
        each(4, cx, lambda p: x_second(p, p, j).wait_recv())

    for t in range(8):
        twin_copy(t, core).wait_send()
        twin_copy(t, 1 - core).wait_recv()


def factor_and_gather(diag, pt):
    w, m = pt.shape
    dma = pltpu.SemaphoreType.DMA
    any_space = pl.BlockSpec(memory_space=pl.ANY)
    vmem = pl.BlockSpec(memory_space=pltpu.VMEM)
    hbm = pl.BlockSpec(memory_space=pltpu.HBM)
    return pl.pallas_call(
        factor_kernel,
        out_shape=(
            jax.ShapeDtypeStruct(diag.shape, F),
            jax.ShapeDtypeStruct((NB, NB), F),
            jax.ShapeDtypeStruct((NB, m), F),
            jax.ShapeDtypeStruct((NB, m), F),
        ),
        in_specs=[hbm, hbm],
        out_specs=[vmem, vmem, any_space, any_space],
        scratch_shapes=[
            pltpu.VMEM(diag.shape, F),
            pltpu.VMEM((w, m), F),
            pltpu.VMEM((w * NB // BLK, BLK), F),
            pltpu.VMEM((NB, w), F),
            pltpu.VMEM((w, m), F),
            pltpu.VMEM((NB, NB), F),
            pltpu.VMEM((NB, NB), F),
            pltpu.VMEM((BLK, NB), F),
        ]
        + [dma((16,))] * 5
        + [dma((4,))] * 5
        + [dma((16,)), dma((16,)), dma((4,)), dma((4,))]
        + [dma((4,)), dma((8,)), dma((8,)), dma((8,)), dma((8,)), dma((2,))],
        compiler_params=pltpu.CompilerParams(
            vmem_limit_bytes=40 << 20, collective_id=0, has_side_effects=True
        ),
    )(diag, pt)


STEP = 256


def update_kernel(l_in, x_ref, pr_ref, pc_ref, slab_ref, l_ref, po_ref, out_ref, xc, cc, buf, rows, sem_in, sem_out):
    m, n = buf.shape
    cut = lambda ref, j: ref.at[j * STEP : (j + 1) * STEP]
    steps = range(m // STEP)
    ins = [pltpu.make_async_copy(cut(slab_ref, j), cut(buf, j), sem_in.at[j]) for j in steps]
    outs = [pltpu.make_async_copy(cut(buf, j), cut(out_ref, j), sem_out.at[j]) for j in steps]
    w = po_ref.shape[0]
    mine = rows.at[pl.ds(pl.multiple_of(lax.axis_index("col") * w, w), w)]
    outs.append(pltpu.make_async_copy(l_in, l_ref, sem_out.at[len(ins)]))
    outs.append(pltpu.make_async_copy(mine, po_ref, sem_out.at[len(ins) + 1]))
    for copy in ins:
        copy.start()
    outs[-2].start()

    def dot(a, b):
        return lax.dot_general(a, b, (NN, ((), ())), preferred_element_type=F)

    h, l = split(x_ref[...])
    xc[:, :NB] = h
    xc[:, NB : 2 * NB] = l
    xc[:, 2 * NB :] = h
    h, l = split(pc_ref[...])
    h, l = split(dot(xc[...], jnp.concatenate([h, h, l], axis=0)))
    cc[:NB] = h
    cc[NB : 2 * NB] = h
    cc[2 * NB :] = l
    h, l = split(pr_ref[...])
    rows[...] = dot(xc[...], jnp.concatenate([h, h, l], axis=0))
    outs[-1].start()
    for j in steps:
        h, l = split(rows[:, j * STEP : (j + 1) * STEP].T)
        product = dot(jnp.concatenate([h, l, h], axis=1), cc[...])
        ins[j].wait()
        buf[j * STEP : (j + 1) * STEP] = buf[j * STEP : (j + 1) * STEP] - product
        outs[j].start()
    for copy in outs:
        copy.wait()


def update(factor, x, pr, pc, slab, w):
    m, n = slab.shape
    vmem = pl.BlockSpec(memory_space=pltpu.VMEM)
    any_space = pl.BlockSpec(memory_space=pl.ANY)
    hbm = pl.BlockSpec(memory_space=pltpu.HBM)
    dma = pltpu.SemaphoreType.DMA
    return pl.pallas_call(
        update_kernel,
        out_shape=(
            jax.ShapeDtypeStruct(factor.shape, F),
            jax.ShapeDtypeStruct((w, m), F),
            jax.ShapeDtypeStruct((m, n), F),
        ),
        in_specs=[vmem, vmem, vmem, vmem, hbm],
        out_specs=[hbm, hbm, hbm],
        scratch_shapes=[
            pltpu.VMEM((NB, 3 * NB), jnp.bfloat16),
            pltpu.VMEM((3 * NB, n), jnp.bfloat16),
            pltpu.VMEM((m, n), F),
            pltpu.VMEM((NB, m), F),
            dma((m // STEP,)),
            dma((m // STEP + 2,)),
        ],
        compiler_params=pltpu.CompilerParams(vmem_limit_bytes=48 << 20),
    )(factor, x, pr, pc, slab)


def body(diag_block, panel, slab):
    in_hbm = lambda v: pltpu.with_memory_space_constraint(v, pltpu.HBM)
    factor, inverse, pr, pc = factor_and_gather(in_hbm(diag_block), in_hbm(panel.T))
    factor_out, panel_out, out = update(factor, inverse, pr, pc, slab, panel.shape[1])
    return factor_out, panel_out.T, out


def solution(mesh):
    spec = P("row", "col")
    return jax.shard_map(
        body, mesh=mesh, in_specs=(spec, spec, spec), out_specs=(spec, spec, spec), check_vma=False
    )
```

```python
import jax
import jax.numpy as jnp
from jax import lax
from jax.sharding import PartitionSpec as P
from jax.experimental import pallas as pl
from jax.experimental.pallas import tpu as pltpu
F=jnp.float32
NB=512; BLK=128

def split(x):
    hi=x.astype(jnp.bfloat16)
    lo=(x-hi.astype(F)).astype(jnp.bfloat16)
    return hi,lo
def dot3(a,b,dims):
    ah,al=split(a); bh,bl=split(b)
    d=lambda x,y: lax.dot_general(x,y,(dims,((),())),preferred_element_type=F)
    return d(ah,bh)+(d(ah,bl)+d(al,bh))
NN=((1,),(0,)); NT=((1,),(1,))

def sweep(tiles, middle):
    lane=lax.broadcasted_iota(jnp.int32,(8,BLK),1)
    sub=lax.broadcasted_iota(jnp.int32,(8,BLK),0)
    n=len(tiles); out=[]
    tiles=list(tiles)
    for p in range(n):
        if p == n // 2:
            middle()
        R=tiles[p]
        rows=[jnp.broadcast_to(R[k:k+1,:],(8,BLK)) for k in range(8)]
        C=[jnp.broadcast_to(R[:,8*p+i:8*p+i+1],(8,BLK)) for i in range(8)]
        B={(k,i):jnp.broadcast_to(C[k][i:i+1,:],(8,BLK)) for k in range(8) for i in range(k,8)}
        inm=(lane>=8*p)&(lane<8*p+8)
        E=[jnp.where(inm,jnp.where(lane==8*p+k,1.0,0.0),rows[k]) for k in range(8)]
        m={}; rcp=[]; rs=[]
        nxt=None
        if p+1<n:
            nc=[jnp.broadcast_to(tiles[p+1][:,8*p+k:8*p+k+1],(8,BLK)) for k in range(8)]
            nxt=jnp.where(inm,0.0,tiles[p+1])
        for k in range(8):
            rc=1.0/B[k,k]; rs.append(lax.rsqrt(B[k,k])); rcp.append(rc)
            for i in range(k+1,8):
                m[i,k]=B[k,i]*rc
            for i in range(k+1,8):
                for j in range(i,8):
                    B[i,j]=B[i,j]-m[i,k]*B[k,j]
                E[i]=E[i]-m[i,k]*E[k]
            if nxt is not None:
                for i in range(k+1,8):
                    nc[i]=nc[i]-m[i,k]*nc[k]
                nxt=nxt-(nc[k]*rc)*E[k]
        V=[None]*8
        for k in reversed(range(8)):
            v=E[k]*rcp[k]
            for i in range(k+1,8):
                v=v-m[i,k]*V[i]
            V[k]=v
        o=E[7]*rs[7]
        for k in range(7):
            o=jnp.where(sub==k,E[k]*rs[k],o)
        out.append(jnp.where(lane<=8*p+sub,o,0.0))
        if nxt is not None: tiles[p+1]=nxt
        for q in range(p+2,n):
            c=[jnp.broadcast_to(tiles[q][:,8*p+k:8*p+k+1],(8,BLK)) for k in range(8)]
            t=jnp.where(inm,0.0,tiles[q])
            acc=[c[k]*V[k] for k in range(8)]
            while len(acc)>1:
                acc=[acc[i]+acc[i+1] for i in range(0,len(acc),2)]
            tiles[q]=t-acc[0]
    return out


MESH = pl.DeviceIdType.MESH


def factor_blocks(a, u, x, s, arrive, middle, rest, hook):
    def step(b, _):
        for bb in range(4):
            o, e = bb * BLK, (bb + 1) * BLK

            @pl.when(b == bb)
            def _():
                arrive(bb)
                if bb == 0:
                    s[:, 0:BLK] = a[0:BLK, 0:BLK]
                else:
                    wt = u[0:o, o:e].T
                    s[:, :o] = -dot3(wt, x[0:o, 0:o], NN)
                    s[:, o:] = a[o:e, o:] - dot3(wt, u[0:o, o:], NN)

        off = pl.multiple_of(b * BLK, BLK)
        out = sweep([s[8 * t : 8 * t + 8, pl.ds(off, BLK)] for t in range(16)], lambda: middle(b))
        for t in range(16):
            x[pl.ds(pl.multiple_of(off + 8 * t, 8), 8), pl.ds(off, BLK)] = out[t]
        for bb in range(4):
            o, e = bb * BLK, (bb + 1) * BLK

            @pl.when(b == bb)
            def _():
                inv = x[o:e, o:e]
                if bb == 0:
                    rest()
                    s[:, BLK:] = a[0:BLK, BLK:]
                u[o:e, o:] = dot3(inv, s[:, o:], NN)
                if bb > 0:
                    x[o:e, :o] = dot3(inv, s[:, :o], NN)
                if bb < 3:
                    x[o:e, e:] = jnp.zeros((BLK, NB - e), F)
                hook(bb)

        return 0

    lax.fori_loop(0, 4, step, 0)


def factor_kernel(
    diag_in, pt_in, l_ref, x_ref, pr_ref, pc_ref, diag_ref, pt_ref, pack, strip, tb, a_ref, u_ref, s_ref,
    s1, r1, s2, r2, s2b, r2b, sx, rx, sy, ry, sx2, rx2, sy2, ry2, st, s5, r5, s6, r6, own,
):
    r = lax.axis_index("row")
    c = lax.axis_index("col")
    n = 16
    w, m = pt_ref.shape
    z = r // 2
    core = lax.rem(r, 2)
    away = lax.rem(r - c + n, n)
    other = r + 1 - 2 * core
    cy, cx = c // 4, lax.rem(c, 4)
    at = lambda i: pl.ds(pl.multiple_of(i * w, w), w)
    at4 = lambda i: pl.ds(pl.multiple_of(i * 4 * w, 4 * w), 4 * w)
    left, right = pl.ds(0, m // 2), pl.ds(m // 2, m // 2)

    def loop(start, stop, fn):
        def step(t, _):
            fn(t)
            return 0

        lax.fori_loop(start, stop, step, 0)

    def each(count, me, fn):
        loop(1, count, lambda t: fn(lax.rem(me + t, count)))

    fetch = [
        pltpu.make_async_copy(diag_in, diag_ref, own.at[0]),
        pltpu.make_async_copy(pt_in, pt_ref, own.at[1]),
    ]
    for copy in fetch:
        copy.start()
    barrier = pltpu.get_barrier_semaphore()

    def greet(row, col):
        pl.semaphore_signal(barrier, 1, device_id=(row, col), device_id_type=MESH)

    each(n, r, lambda p: greet(p, c))
    each(n, c, lambda p: greet(r, p))
    pl.semaphore_wait(barrier, 2 * (n - 1))

    def remote(src, dst, send, recv, row, col):
        return pltpu.make_async_remote_copy(src, dst, send, recv, device_id=(row, col), device_id_type=MESH)

    pw = pack.shape[0] // n
    at8 = lambda i: pl.ds(pl.multiple_of(i * pw, pw), pw)

    def diag_copy(src, peer):
        part = pack.at[at8(src), :]
        return remote(part, part, s1.at[peer], r1.at[src], peer, c)

    def strip_copy(src, peer, q):
        part = a_ref.at[at(src), q * BLK :] if q else a_ref.at[at(src), 0:BLK]
        return remote(part, part, s2.at[peer], r2.at[src], r, peer)

    def rest_copy(src, peer):
        part = a_ref.at[at(src), BLK:]
        return remote(part, part, s2b.at[peer], r2b.at[src], r, peer)

    def x_first(src, peer):
        return remote(pt_ref.at[:, left], pr_ref.at[at(4 * cy + src), left], sx.at[peer], rx.at[src], r, 4 * cy + peer)

    def y_first(src, peer):
        return remote(pt_ref.at[:, right], pr_ref.at[at(4 * src + cx), right], sy.at[peer], ry.at[src], r, 4 * peer + cx)

    def y_second(src, peer):
        part = pr_ref.at[at4(src), left]
        return remote(part, part, sy2.at[peer], ry2.at[src], r, 4 * peer + cx)

    def x_second(src, peer, j):
        part = pr_ref.at[at(4 * j + src), right]
        return remote(part, part, sx2.at[4 * peer + j], rx2.at[4 * src + j], r, 4 * cy + peer)

    def turn_z():
        return remote(pt_ref, tb, st.at[0], st.at[1], lax.rem(r + c, n), c)

    def turn_plane():
        return remote(tb, pc_ref.at[at(c), :], st.at[2], st.at[3], r, away)

    def turn_plane_in():
        return remote(tb, pc_ref.at[at(away), :], st.at[2], st.at[3], r, away)

    def turn_local(src, dst):
        return pltpu.make_async_copy(src, dst, own.at[1])

    def z_row(t):
        return 2 * lax.rem(z + t + 8, 8) + core

    def piece(t, side):
        return pc_ref.at[at(lax.rem(2 * lax.rem(z + t + 8, 8) + side - c + n, n)), :]

    def z_copy(i, src, to):
        part = piece(src, core)
        return remote(part, part, s5.at[i], r5.at[(src - to) % 8], z_row(to), c)

    def z_in(src):
        part = piece(src, core)
        return remote(part, part, s5.at[0], r5.at[src % 8], r, c)

    def twin_copy(t, side):
        part = piece(t, side)
        return remote(part, part, s6.at[t % 8], r6.at[t % 8], other, c)

    first = ((0, 2), (0, -2), (0, 1), (0, -1))
    relay = ((-2, 2), (-2, 1), (2, -1))

    fetch[0].wait()
    block = diag_ref[...]
    pack[at8(r), :] = jnp.concatenate([block[pw * j : pw * j + pw, :] for j in range(w // pw)], axis=1)
    each(n, r, lambda p: diag_copy(r, p).start())
    fetch[1].wait()
    keep = pltpu.make_async_copy(pt_ref, pr_ref.at[at(c), :], own.at[0])
    keep.start()

    @pl.when(c != 0)
    def _():
        turn_z().start()

    @pl.when(c == 0)
    def _():
        turn_local(pt_ref, tb).start()

    each(n, r, lambda p: diag_copy(p, p).wait_recv())
    for i in range(n):
        packed = pack[pw * i : pw * i + pw, :]
        for j in range(w // pw):
            moved = packed if j == 0 else pltpu.roll(packed, BLK - w * j, 1)
            strip[w * i + pw * j : w * i + pw * j + pw, :] = moved[:, :w]
    a_ref[at(c), :] = strip[...].T
    group = c // 4

    def strips(fn, groups):
        for q in groups:

            @pl.when(group == q)
            def _():
                each(n, c, lambda p: fn(p, q))

    strips(lambda p, q: strip_copy(c, p, q).start(), (0,))

    @pl.when(c != 0)
    def _():
        turn_z().wait()

    @pl.when(c == 0)
    def _():
        turn_local(pt_ref, tb).wait()

    @pl.when(away != c)
    def _():
        turn_plane().start()

    @pl.when(away == c)
    def _():
        turn_local(tb, pc_ref.at[at(c), :]).start()

    strips(lambda p, q: rest_copy(c, p).start(), (0,))
    strips(lambda p, q: strip_copy(c, p, q).start(), (1, 2, 3))

    def arrive(bb):
        def one(t):
            @pl.when(t != c)
            def _():
                strip_copy(t, t, bb).wait_recv()

        loop(4 * bb, 4 * bb + 4, one)
        if bb == 0:
            each(4, cx, lambda p: x_first(cx, p).start())
            each(4, cy, lambda p: y_first(cy, p).start())

    def middle(b):
        @pl.when(b == 0)
        def _():
            @pl.when(away != c)
            def _():
                turn_plane_in().wait()

            @pl.when(away == c)
            def _():
                turn_local(tb, pc_ref.at[at(c), :]).wait()

            for i, (src, to) in enumerate(first):
                z_copy(i, src, to).start()
            twin_copy(0, core).start()

        @pl.when(b == 1)
        def _():
            z_in(-2).wait_recv()
            z_in(2).wait_recv()
            for i, (src, to) in enumerate(relay):
                z_copy(4 + i, src, to).start()
            for t in (2, -2):
                twin_copy(t, core).start()

        @pl.when(b == 2)
        def _():
            for t in (1, -1):
                z_in(t).wait_recv()
                twin_copy(t, core).start()

        @pl.when(b == 3)
        def _():
            for t in (4, 3, -3):
                z_in(t).wait_recv()
                twin_copy(t, core).start()

    def rest():
        def one(t):
            @pl.when(t != c)
            def _():
                rest_copy(t, t).wait_recv()

        loop(0, 4, one)

    def hook(bb):
        if bb == 0:
            keep.wait()
            each(4, cx, lambda p: x_first(p, p).wait_recv())
            each(4, cy, lambda p: y_second(cy, p).start())
            each(4, cy, lambda p: y_first(p, p).wait_recv())
            for j in range(4):
                each(4, cx, lambda p: x_second(cx, p, j).start())

    factor_blocks(a_ref, u_ref, x_ref, s_ref, arrive, middle, rest, hook)

    rows, cols = l_ref.shape
    per = BLK // w
    chunk = u_ref[at(c), pl.ds(pl.multiple_of((r // per) * BLK, BLK), BLK)]
    turned = pltpu.roll(chunk, lax.rem(BLK - lax.rem(r, per) * w, BLK), 1)[:, :w].T
    gi = r * w + lax.broadcasted_iota(jnp.int32, (rows, cols), 0)
    gj = c * w + lax.broadcasted_iota(jnp.int32, (rows, cols), 1)
    l_ref[...] = jnp.where(gi >= gj, turned, 0.0)

    each(n, r, lambda p: diag_copy(r, p).wait_send())
    strips(lambda p, q: rest_copy(c, p).wait_send(), (0,))
    strips(lambda p, q: strip_copy(c, p, q).wait_send(), (0, 1, 2, 3))
    each(4, cx, lambda p: x_first(cx, p).wait_send())
    each(4, cy, lambda p: y_first(cy, p).wait_send())
    for i, (src, to) in enumerate(first + relay):
        z_copy(i, src, to).wait_send()
    each(4, cy, lambda p: y_second(cy, p).wait_send())
    each(4, cy, lambda p: y_second(p, p).wait_recv())
    for j in range(4):
        each(4, cx, lambda p: x_second(cx, p, j).wait_send())
        each(4, cx, lambda p: x_second(p, p, j).wait_recv())

    for t in range(8):
        twin_copy(t, core).wait_send()
        twin_copy(t, 1 - core).wait_recv()


def factor_and_gather(diag, pt):
    w, m = pt.shape
    dma = pltpu.SemaphoreType.DMA
    any_space = pl.BlockSpec(memory_space=pl.ANY)
    vmem = pl.BlockSpec(memory_space=pltpu.VMEM)
    hbm = pl.BlockSpec(memory_space=pltpu.HBM)
    return pl.pallas_call(
        factor_kernel,
        out_shape=(
            jax.ShapeDtypeStruct(diag.shape, F),
            jax.ShapeDtypeStruct((NB, NB), F),
            jax.ShapeDtypeStruct((NB, m), F),
            jax.ShapeDtypeStruct((NB, m), F),
        ),
        in_specs=[hbm, hbm],
        out_specs=[vmem, vmem, any_space, any_space],
        scratch_shapes=[
            pltpu.VMEM(diag.shape, F),
            pltpu.VMEM((w, m), F),
            pltpu.VMEM((w * NB // BLK, BLK), F),
            pltpu.VMEM((NB, w), F),
            pltpu.VMEM((w, m), F),
            pltpu.VMEM((NB, NB), F),
            pltpu.VMEM((NB, NB), F),
            pltpu.VMEM((BLK, NB), F),
        ]
        + [dma((16,))] * 5
        + [dma((4,))] * 5
        + [dma((16,)), dma((16,)), dma((4,)), dma((4,))]
        + [dma((4,)), dma((8,)), dma((8,)), dma((8,)), dma((8,)), dma((2,))],
        compiler_params=pltpu.CompilerParams(
            vmem_limit_bytes=40 << 20, collective_id=0, has_side_effects=True
        ),
    )(diag, pt)


STEP = 256


def update_kernel(l_in, x_ref, pr_ref, pc_ref, slab_ref, l_ref, po_ref, out_ref, xc, cc, buf, rows, sem_in, sem_out):
    m, n = buf.shape
    cut = lambda ref, j: ref.at[j * STEP : (j + 1) * STEP]
    steps = range(m // STEP)
    ins = [pltpu.make_async_copy(cut(slab_ref, j), cut(buf, j), sem_in.at[j]) for j in steps]
    outs = [pltpu.make_async_copy(cut(buf, j), cut(out_ref, j), sem_out.at[j]) for j in steps]
    w = po_ref.shape[0]
    mine = rows.at[pl.ds(pl.multiple_of(lax.axis_index("col") * w, w), w)]
    outs.append(pltpu.make_async_copy(l_in, l_ref, sem_out.at[len(ins)]))
    outs.append(pltpu.make_async_copy(mine, po_ref, sem_out.at[len(ins) + 1]))
    for copy in ins:
        copy.start()
    outs[-2].start()

    def dot(a, b):
        return lax.dot_general(a, b, (NN, ((), ())), preferred_element_type=F)

    h, l = split(x_ref[...])
    xc[:, :NB] = h
    xc[:, NB : 2 * NB] = l
    xc[:, 2 * NB :] = h
    h, l = split(pc_ref[...])
    h, l = split(dot(xc[...], jnp.concatenate([h, h, l], axis=0)))
    cc[:NB] = h
    cc[NB : 2 * NB] = h
    cc[2 * NB :] = l
    h, l = split(pr_ref[...])
    rows[...] = dot(xc[...], jnp.concatenate([h, h, l], axis=0))
    outs[-1].start()
    for j in steps:
        h, l = split(rows[:, j * STEP : (j + 1) * STEP].T)
        product = dot(jnp.concatenate([h, l, h], axis=1), cc[...])
        ins[j].wait()
        buf[j * STEP : (j + 1) * STEP] = buf[j * STEP : (j + 1) * STEP] - product
        outs[j].start()
    for copy in outs:
        copy.wait()


def update(factor, x, pr, pc, slab, w):
    m, n = slab.shape
    vmem = pl.BlockSpec(memory_space=pltpu.VMEM)
    any_space = pl.BlockSpec(memory_space=pl.ANY)
    hbm = pl.BlockSpec(memory_space=pltpu.HBM)
    dma = pltpu.SemaphoreType.DMA
    return pl.pallas_call(
        update_kernel,
        out_shape=(
            jax.ShapeDtypeStruct(factor.shape, F),
            jax.ShapeDtypeStruct((w, m), F),
            jax.ShapeDtypeStruct((m, n), F),
        ),
        in_specs=[vmem, vmem, vmem, vmem, hbm],
        out_specs=[hbm, hbm, hbm],
        scratch_shapes=[
            pltpu.VMEM((NB, 3 * NB), jnp.bfloat16),
            pltpu.VMEM((3 * NB, n), jnp.bfloat16),
            pltpu.VMEM((m, n), F),
            pltpu.VMEM((NB, m), F),
            dma((m // STEP,)),
            dma((m // STEP + 2,)),
        ],
        compiler_params=pltpu.CompilerParams(vmem_limit_bytes=48 << 20),
    )(factor, x, pr, pc, slab)


def body(diag_block, panel, slab):
    in_hbm = lambda v: pltpu.with_memory_space_constraint(v, pltpu.HBM)
    factor, inverse, pr, pc = factor_and_gather(in_hbm(diag_block), in_hbm(panel.T))
    factor_out, panel_out, out = update(factor, inverse, pr, pc, slab, panel.shape[1])
    return factor_out, panel_out.T, out


def solution(mesh):
    spec = P("row", "col")
    return jax.shard_map(
        body, mesh=mesh, in_specs=(spec, spec, spec), out_specs=(spec, spec, spec), check_vma=False
    )
```

```python
import jax
import jax.numpy as jnp
from jax import lax
from jax.sharding import PartitionSpec as P
from jax.experimental import pallas as pl
from jax.experimental.pallas import tpu as pltpu
F=jnp.float32
NB=512; BLK=128

def split(x):
    hi=x.astype(jnp.bfloat16)
    lo=(x-hi.astype(F)).astype(jnp.bfloat16)
    return hi,lo
def dot3(a,b,dims):
    ah,al=split(a); bh,bl=split(b)
    d=lambda x,y: lax.dot_general(x,y,(dims,((),())),preferred_element_type=F)
    return d(ah,bh)+(d(ah,bl)+d(al,bh))
NN=((1,),(0,)); NT=((1,),(1,))

def sweep(tiles, middle):
    lane=lax.broadcasted_iota(jnp.int32,(8,BLK),1)
    sub=lax.broadcasted_iota(jnp.int32,(8,BLK),0)
    n=len(tiles); out=[]
    tiles=list(tiles)
    for p in range(n):
        if p == n // 2:
            middle()
        R=tiles[p]
        rows=[jnp.broadcast_to(R[k:k+1,:],(8,BLK)) for k in range(8)]
        C=[jnp.broadcast_to(R[:,8*p+i:8*p+i+1],(8,BLK)) for i in range(8)]
        B={(k,i):jnp.broadcast_to(C[k][i:i+1,:],(8,BLK)) for k in range(8) for i in range(k,8)}
        inm=(lane>=8*p)&(lane<8*p+8)
        E=[jnp.where(inm,jnp.where(lane==8*p+k,1.0,0.0),rows[k]) for k in range(8)]
        m={}; rcp=[]; rs=[]
        nxt=None
        if p+1<n:
            nc=[jnp.broadcast_to(tiles[p+1][:,8*p+k:8*p+k+1],(8,BLK)) for k in range(8)]
            nxt=jnp.where(inm,0.0,tiles[p+1])
        for k in range(8):
            rc=1.0/B[k,k]; rs.append(lax.rsqrt(B[k,k])); rcp.append(rc)
            for i in range(k+1,8):
                m[i,k]=B[k,i]*rc
            for i in range(k+1,8):
                for j in range(i,8):
                    B[i,j]=B[i,j]-m[i,k]*B[k,j]
                E[i]=E[i]-m[i,k]*E[k]
            if nxt is not None:
                for i in range(k+1,8):
                    nc[i]=nc[i]-m[i,k]*nc[k]
                nxt=nxt-(nc[k]*rc)*E[k]
        V=[None]*8
        for k in reversed(range(8)):
            v=E[k]*rcp[k]
            for i in range(k+1,8):
                v=v-m[i,k]*V[i]
            V[k]=v
        o=E[7]*rs[7]
        for k in range(7):
            o=jnp.where(sub==k,E[k]*rs[k],o)
        out.append(jnp.where(lane<=8*p+sub,o,0.0))
        if nxt is not None: tiles[p+1]=nxt
        for q in range(p+2,n):
            c=[jnp.broadcast_to(tiles[q][:,8*p+k:8*p+k+1],(8,BLK)) for k in range(8)]
            t=jnp.where(inm,0.0,tiles[q])
            acc=[c[k]*V[k] for k in range(8)]
            while len(acc)>1:
                acc=[acc[i]+acc[i+1] for i in range(0,len(acc),2)]
            tiles[q]=t-acc[0]
    return out


MESH = pl.DeviceIdType.MESH


def factor_blocks(a, u, x, s, arrive, middle, rest, hook):
    def step(b, _):
        for bb in range(4):
            o, e = bb * BLK, (bb + 1) * BLK

            @pl.when(b == bb)
            def _():
                arrive(bb)
                if bb == 0:
                    s[:, 0:BLK] = a[0:BLK, 0:BLK]
                else:
                    wt = u[0:o, o:e].T
                    s[:, :o] = -dot3(wt, x[0:o, 0:o], NN)
                    s[:, o:] = a[o:e, o:] - dot3(wt, u[0:o, o:], NN)

        off = pl.multiple_of(b * BLK, BLK)
        out = sweep([s[8 * t : 8 * t + 8, pl.ds(off, BLK)] for t in range(16)], lambda: middle(b))
        for t in range(16):
            x[pl.ds(pl.multiple_of(off + 8 * t, 8), 8), pl.ds(off, BLK)] = out[t]
        for bb in range(4):
            o, e = bb * BLK, (bb + 1) * BLK

            @pl.when(b == bb)
            def _():
                inv = x[o:e, o:e]
                if bb == 0:
                    rest()
                    s[:, BLK:] = a[0:BLK, BLK:]
                u[o:e, o:] = dot3(inv, s[:, o:], NN)
                if bb > 0:
                    x[o:e, :o] = dot3(inv, s[:, :o], NN)
                if bb < 3:
                    x[o:e, e:] = jnp.zeros((BLK, NB - e), F)
                hook(bb)

        return 0

    lax.fori_loop(0, 4, step, 0)


def factor_kernel(
    diag_in, pt_in, l_ref, x_ref, pr_ref, pc_ref, diag_ref, pt_ref, pack, strip, tb, a_ref, u_ref, s_ref,
    s1, r1, s2, r2, s2b, r2b, sx, rx, sy, ry, sx2, rx2, sy2, ry2, st, s5, r5, s6, r6, own,
):
    r = lax.axis_index("row")
    c = lax.axis_index("col")
    n = 16
    w, m = pt_ref.shape
    z = r // 2
    core = lax.rem(r, 2)
    away = lax.rem(r - c + n, n)
    other = r + 1 - 2 * core
    cy, cx = c // 4, lax.rem(c, 4)
    at = lambda i: pl.ds(pl.multiple_of(i * w, w), w)
    at4 = lambda i: pl.ds(pl.multiple_of(i * 4 * w, 4 * w), 4 * w)
    left, right = pl.ds(0, m // 2), pl.ds(m // 2, m // 2)

    def loop(start, stop, fn):
        def step(t, _):
            fn(t)
            return 0

        lax.fori_loop(start, stop, step, 0)

    def each(count, me, fn):
        loop(1, count, lambda t: fn(lax.rem(me + t, count)))

    fetch = [
        pltpu.make_async_copy(diag_in, diag_ref, own.at[0]),
        pltpu.make_async_copy(pt_in, pt_ref, own.at[1]),
    ]
    for copy in fetch:
        copy.start()
    barrier = pltpu.get_barrier_semaphore()

    def greet(row, col):
        pl.semaphore_signal(barrier, 1, device_id=(row, col), device_id_type=MESH)

    each(n, r, lambda p: greet(p, c))
    each(n, c, lambda p: greet(r, p))
    pl.semaphore_wait(barrier, 2 * (n - 1))

    def remote(src, dst, send, recv, row, col):
        return pltpu.make_async_remote_copy(src, dst, send, recv, device_id=(row, col), device_id_type=MESH)

    def wait_all(part, send, recv, sent):
        every = remote(part, part, send, recv, r, c)
        if sent:
            every.wait_send()
        else:
            every.wait_recv()

    pw = pack.shape[0] // n
    at8 = lambda i: pl.ds(pl.multiple_of(i * pw, pw), pw)

    def diag_copy(src, peer):
        part = pack.at[at8(src), :]
        return remote(part, part, s1, r1, peer, c)

    def strip_copy(src, peer, q):
        part = a_ref.at[at(src), q * BLK :] if q else a_ref.at[at(src), 0:BLK]
        return remote(part, part, s2, r2.at[src], r, peer)

    def rest_copy(src, peer):
        part = a_ref.at[at(src), BLK:]
        return remote(part, part, s2b, r2b.at[src], r, peer)

    def x_first(src, peer):
        return remote(pt_ref.at[:, left], pr_ref.at[at(4 * cy + src), left], sx, rx, r, 4 * cy + peer)

    def y_first(src, peer):
        return remote(pt_ref.at[:, right], pr_ref.at[at(4 * src + cx), right], sy, ry, r, 4 * peer + cx)

    def y_second(src, peer):
        part = pr_ref.at[at4(src), left]
        return remote(part, part, sy2, ry2, r, 4 * peer + cx)

    def x_second(src, peer, j):
        part = pr_ref.at[at(4 * j + src), right]
        return remote(part, part, sx2, rx2, r, 4 * cy + peer)

    def turn_z():
        return remote(pt_ref, tb, st.at[0], st.at[1], lax.rem(r + c, n), c)

    def turn_plane():
        return remote(tb, pc_ref.at[at(c), :], st.at[2], st.at[3], r, away)

    def turn_plane_in():
        return remote(tb, pc_ref.at[at(away), :], st.at[2], st.at[3], r, away)

    def turn_local(src, dst):
        return pltpu.make_async_copy(src, dst, own.at[1])

    def z_row(t):
        return 2 * lax.rem(z + t + 8, 8) + core

    def piece(t, side):
        return pc_ref.at[at(lax.rem(2 * lax.rem(z + t + 8, 8) + side - c + n, n)), :]

    def z_copy(i, src, to):
        part = piece(src, core)
        return remote(part, part, s5, r5.at[(src - to) % 8], z_row(to), c)

    def z_in(src):
        part = piece(src, core)
        return remote(part, part, s5, r5.at[src % 8], r, c)

    def twin_copy(t, side):
        part = piece(t, side)
        return remote(part, part, s6, r6, other, c)

    first = ((0, 2), (0, -2), (0, 1), (0, -1))
    relay = ((-2, 2), (-2, 1), (2, -1))

    fetch[0].wait()
    block = diag_ref[...]
    pack[at8(r), :] = jnp.concatenate([block[pw * j : pw * j + pw, :] for j in range(w // pw)], axis=1)
    each(n, r, lambda p: diag_copy(r, p).start())
    fetch[1].wait()
    keep = pltpu.make_async_copy(pt_ref, pr_ref.at[at(c), :], own.at[0])
    keep.start()

    @pl.when(c != 0)
    def _():
        turn_z().start()

    @pl.when(c == 0)
    def _():
        turn_local(pt_ref, tb).start()

    wait_all(pack.at[0 : (n - 1) * pw], s1, r1, False)
    for i in range(n):
        packed = pack[pw * i : pw * i + pw, :]
        for j in range(w // pw):
            moved = packed if j == 0 else pltpu.roll(packed, BLK - w * j, 1)
            strip[w * i + pw * j : w * i + pw * j + pw, :] = moved[:, :w]
    a_ref[at(c), :] = strip[...].T
    group = c // 4

    def strips(fn, groups):
        for q in groups:

            @pl.when(group == q)
            def _():
                each(n, c, lambda p: fn(p, q))

    strips(lambda p, q: strip_copy(c, p, q).start(), (0,))

    @pl.when(c != 0)
    def _():
        turn_z().wait()

    @pl.when(c == 0)
    def _():
        turn_local(pt_ref, tb).wait()

    @pl.when(away != c)
    def _():
        turn_plane().start()

    @pl.when(away == c)
    def _():
        turn_local(tb, pc_ref.at[at(c), :]).start()

    strips(lambda p, q: rest_copy(c, p).start(), (0,))
    strips(lambda p, q: strip_copy(c, p, q).start(), (1, 2, 3))

    def arrive(bb):
        def one(t):
            @pl.when(t != c)
            def _():
                strip_copy(t, t, bb).wait_recv()

        loop(4 * bb, 4 * bb + 4, one)
        if bb == 0:
            each(4, cx, lambda p: x_first(cx, p).start())
            each(4, cy, lambda p: y_first(cy, p).start())

    def middle(b):
        @pl.when(b == 0)
        def _():
            @pl.when(away != c)
            def _():
                turn_plane_in().wait()

            @pl.when(away == c)
            def _():
                turn_local(tb, pc_ref.at[at(c), :]).wait()

            for i, (src, to) in enumerate(first):
                z_copy(i, src, to).start()
            twin_copy(0, core).start()

        @pl.when(b == 1)
        def _():
            z_in(-2).wait_recv()
            z_in(2).wait_recv()
            for i, (src, to) in enumerate(relay):
                z_copy(4 + i, src, to).start()
            for t in (2, -2):
                twin_copy(t, core).start()

        @pl.when(b == 2)
        def _():
            for t in (1, -1):
                z_in(t).wait_recv()
                twin_copy(t, core).start()

        @pl.when(b == 3)
        def _():
            for t in (4, 3, -3):
                z_in(t).wait_recv()
                twin_copy(t, core).start()

    def rest():
        def one(t):
            @pl.when(t != c)
            def _():
                rest_copy(t, t).wait_recv()

        loop(0, 4, one)

    def hook(bb):
        if bb == 0:
            keep.wait()
            wait_all(pr_ref.at[0 : 3 * w, left], sx, rx, False)
            each(4, cy, lambda p: y_second(cy, p).start())
            wait_all(pr_ref.at[0 : 3 * w, right], sy, ry, False)
            for j in range(4):
                each(4, cx, lambda p: x_second(cx, p, j).start())

    factor_blocks(a_ref, u_ref, x_ref, s_ref, arrive, middle, rest, hook)

    rows, cols = l_ref.shape
    per = BLK // w
    chunk = u_ref[at(c), pl.ds(pl.multiple_of((r // per) * BLK, BLK), BLK)]
    turned = pltpu.roll(chunk, lax.rem(BLK - lax.rem(r, per) * w, BLK), 1)[:, :w].T
    gi = r * w + lax.broadcasted_iota(jnp.int32, (rows, cols), 0)
    gj = c * w + lax.broadcasted_iota(jnp.int32, (rows, cols), 1)
    l_ref[...] = jnp.where(gi >= gj, turned, 0.0)

    wait_all(pack.at[0 : (n - 1) * pw], s1, r1, True)
    for q in range(4):

        @pl.when(group == q)
        def _():
            if q == 0:
                wait_all(a_ref.at[0 : (n - 1) * w, 0:BLK], s2, r2.at[0], True)
                wait_all(a_ref.at[0 : (n - 1) * w, BLK:], s2b, r2b.at[0], True)
            else:
                wait_all(a_ref.at[0 : (n - 1) * w, q * BLK :], s2, r2.at[0], True)

    wait_all(pr_ref.at[0 : 3 * w, left], sx, rx, True)
    wait_all(pr_ref.at[0 : 3 * w, right], sy, ry, True)
    wait_all(pc_ref.at[0 : 7 * w, :], s5, r5.at[0], True)
    for sent in (True, False):
        wait_all(pr_ref.at[0 : 12 * w, left], sy2, ry2, sent)
        wait_all(pr_ref.at[0 : 12 * w, right], sx2, rx2, sent)
        wait_all(pc_ref.at[0 : 8 * w, :], s6, r6, sent)


def factor_and_gather(diag, pt):
    w, m = pt.shape
    dma = pltpu.SemaphoreType.DMA
    any_space = pl.BlockSpec(memory_space=pl.ANY)
    vmem = pl.BlockSpec(memory_space=pltpu.VMEM)
    hbm = pl.BlockSpec(memory_space=pltpu.HBM)
    return pl.pallas_call(
        factor_kernel,
        out_shape=(
            jax.ShapeDtypeStruct(diag.shape, F),
            jax.ShapeDtypeStruct((NB, NB), F),
            jax.ShapeDtypeStruct((NB, m), F),
            jax.ShapeDtypeStruct((NB, m), F),
        ),
        in_specs=[hbm, hbm],
        out_specs=[vmem, vmem, any_space, any_space],
        scratch_shapes=[
            pltpu.VMEM(diag.shape, F),
            pltpu.VMEM((w, m), F),
            pltpu.VMEM((w * NB // BLK, BLK), F),
            pltpu.VMEM((NB, w), F),
            pltpu.VMEM((w, m), F),
            pltpu.VMEM((NB, NB), F),
            pltpu.VMEM((NB, NB), F),
            pltpu.VMEM((BLK, NB), F),
        ]
        + [dma(()), dma(()), dma(()), dma((16,)), dma(()), dma((4,)), dma(()), dma(()), dma(()), dma(()), dma(()), dma(()), dma(()), dma(()), dma((4,)), dma(()), dma((8,)), dma(()), dma(()), dma((2,))],
        compiler_params=pltpu.CompilerParams(
            vmem_limit_bytes=40 << 20, collective_id=0, has_side_effects=True
        ),
    )(diag, pt)


STEP = 256


def update_kernel(l_in, x_ref, pr_ref, pc_ref, slab_ref, l_ref, po_ref, out_ref, xc, cc, buf, rows, sem_in, sem_out):
    m, n = buf.shape
    cut = lambda ref, j: ref.at[j * STEP : (j + 1) * STEP]
    steps = range(m // STEP)
    ins = [pltpu.make_async_copy(cut(slab_ref, j), cut(buf, j), sem_in.at[j]) for j in steps]
    outs = [pltpu.make_async_copy(cut(buf, j), cut(out_ref, j), sem_out.at[j]) for j in steps]
    w = po_ref.shape[0]
    mine = rows.at[pl.ds(pl.multiple_of(lax.axis_index("col") * w, w), w)]
    outs.append(pltpu.make_async_copy(l_in, l_ref, sem_out.at[len(ins)]))
    outs.append(pltpu.make_async_copy(mine, po_ref, sem_out.at[len(ins) + 1]))
    for copy in ins:
        copy.start()
    outs[-2].start()

    def dot(a, b):
        return lax.dot_general(a, b, (NN, ((), ())), preferred_element_type=F)

    h, l = split(x_ref[...])
    xc[:, :NB] = h
    xc[:, NB : 2 * NB] = l
    xc[:, 2 * NB :] = h
    h, l = split(pc_ref[...])
    h, l = split(dot(xc[...], jnp.concatenate([h, h, l], axis=0)))
    cc[:NB] = h
    cc[NB : 2 * NB] = h
    cc[2 * NB :] = l
    h, l = split(pr_ref[...])
    rows[...] = dot(xc[...], jnp.concatenate([h, h, l], axis=0))
    outs[-1].start()
    for j in steps:
        h, l = split(rows[:, j * STEP : (j + 1) * STEP].T)
        product = dot(jnp.concatenate([h, l, h], axis=1), cc[...])
        ins[j].wait()
        buf[j * STEP : (j + 1) * STEP] = buf[j * STEP : (j + 1) * STEP] - product
        outs[j].start()
    for copy in outs:
        copy.wait()


def update(factor, x, pr, pc, slab, w):
    m, n = slab.shape
    vmem = pl.BlockSpec(memory_space=pltpu.VMEM)
    any_space = pl.BlockSpec(memory_space=pl.ANY)
    hbm = pl.BlockSpec(memory_space=pltpu.HBM)
    dma = pltpu.SemaphoreType.DMA
    return pl.pallas_call(
        update_kernel,
        out_shape=(
            jax.ShapeDtypeStruct(factor.shape, F),
            jax.ShapeDtypeStruct((w, m), F),
            jax.ShapeDtypeStruct((m, n), F),
        ),
        in_specs=[vmem, vmem, vmem, vmem, hbm],
        out_specs=[hbm, hbm, hbm],
        scratch_shapes=[
            pltpu.VMEM((NB, 3 * NB), jnp.bfloat16),
            pltpu.VMEM((3 * NB, n), jnp.bfloat16),
            pltpu.VMEM((m, n), F),
            pltpu.VMEM((NB, m), F),
            dma((m // STEP,)),
            dma((m // STEP + 2,)),
        ],
        compiler_params=pltpu.CompilerParams(vmem_limit_bytes=48 << 20),
    )(factor, x, pr, pc, slab)


def body(diag_block, panel, slab):
    in_hbm = lambda v: pltpu.with_memory_space_constraint(v, pltpu.HBM)
    factor, inverse, pr, pc = factor_and_gather(in_hbm(diag_block), in_hbm(panel.T))
    factor_out, panel_out, out = update(factor, inverse, pr, pc, slab, panel.shape[1])
    return factor_out, panel_out.T, out


def solution(mesh):
    spec = P("row", "col")
    return jax.shard_map(
        body, mesh=mesh, in_specs=(spec, spec, spec), out_specs=(spec, spec, spec), check_vma=False
    )
```

```python
import jax
import jax.numpy as jnp
from jax import lax
from jax.sharding import PartitionSpec as P
from jax.experimental import pallas as pl
from jax.experimental.pallas import tpu as pltpu
F=jnp.float32
NB=512; BLK=128

def split(x):
    hi=x.astype(jnp.bfloat16)
    lo=(x-hi.astype(F)).astype(jnp.bfloat16)
    return hi,lo
def dot3(a,b,dims):
    ah,al=split(a); bh,bl=split(b)
    d=lambda x,y: lax.dot_general(x,y,(dims,((),())),preferred_element_type=F)
    return d(ah,bh)+(d(ah,bl)+d(al,bh))
NN=((1,),(0,)); NT=((1,),(1,))

def sweep(tiles, middle):
    lane=lax.broadcasted_iota(jnp.int32,(8,BLK),1)
    sub=lax.broadcasted_iota(jnp.int32,(8,BLK),0)
    n=len(tiles); out=[]
    tiles=list(tiles)
    for p in range(n):
        if p == 5 * n // 8:
            middle()
        R=tiles[p]
        rows=[jnp.broadcast_to(R[k:k+1,:],(8,BLK)) for k in range(8)]
        C=[jnp.broadcast_to(R[:,8*p+i:8*p+i+1],(8,BLK)) for i in range(8)]
        B={(k,i):jnp.broadcast_to(C[k][i:i+1,:],(8,BLK)) for k in range(8) for i in range(k,8)}
        inm=(lane>=8*p)&(lane<8*p+8)
        E=[jnp.where(inm,jnp.where(lane==8*p+k,1.0,0.0),rows[k]) for k in range(8)]
        m={}; rcp=[]; rs=[]
        nxt=None
        if p+1<n:
            nc=[jnp.broadcast_to(tiles[p+1][:,8*p+k:8*p+k+1],(8,BLK)) for k in range(8)]
            nxt=jnp.where(inm,0.0,tiles[p+1])
        for k in range(8):
            rc=1.0/B[k,k]; rs.append(lax.rsqrt(B[k,k])); rcp.append(rc)
            for i in range(k+1,8):
                m[i,k]=B[k,i]*rc
            for i in range(k+1,8):
                for j in range(i,8):
                    B[i,j]=B[i,j]-m[i,k]*B[k,j]
                E[i]=E[i]-m[i,k]*E[k]
            if nxt is not None:
                for i in range(k+1,8):
                    nc[i]=nc[i]-m[i,k]*nc[k]
                nxt=nxt-(nc[k]*rc)*E[k]
        V=[None]*8
        for k in reversed(range(8)):
            v=E[k]*rcp[k]
            for i in range(k+1,8):
                v=v-m[i,k]*V[i]
            V[k]=v
        o=E[7]*rs[7]
        for k in range(7):
            o=jnp.where(sub==k,E[k]*rs[k],o)
        out.append(jnp.where(lane<=8*p+sub,o,0.0))
        if nxt is not None: tiles[p+1]=nxt
        for q in range(p+2,n):
            c=[jnp.broadcast_to(tiles[q][:,8*p+k:8*p+k+1],(8,BLK)) for k in range(8)]
            t=jnp.where(inm,0.0,tiles[q])
            acc=[c[k]*V[k] for k in range(8)]
            while len(acc)>1:
                acc=[acc[i]+acc[i+1] for i in range(0,len(acc),2)]
            tiles[q]=t-acc[0]
    return out


MESH = pl.DeviceIdType.MESH


def factor_blocks(a, u, x, s, arrive, middle, rest, hook):
    def step(b, _):
        for bb in range(4):
            o, e = bb * BLK, (bb + 1) * BLK

            @pl.when(b == bb)
            def _():
                arrive(bb)
                if bb == 0:
                    s[:, 0:BLK] = a[0:BLK, 0:BLK]
                else:
                    wt = u[0:o, o:e].T
                    s[:, :o] = -dot3(wt, x[0:o, 0:o], NN)
                    s[:, o:] = a[o:e, o:] - dot3(wt, u[0:o, o:], NN)

        off = pl.multiple_of(b * BLK, BLK)
        out = sweep([s[8 * t : 8 * t + 8, pl.ds(off, BLK)] for t in range(16)], lambda: middle(b))
        for t in range(16):
            x[pl.ds(pl.multiple_of(off + 8 * t, 8), 8), pl.ds(off, BLK)] = out[t]
        for bb in range(4):
            o, e = bb * BLK, (bb + 1) * BLK

            @pl.when(b == bb)
            def _():
                inv = x[o:e, o:e]
                if bb == 0:
                    rest()
                    s[:, BLK:] = a[0:BLK, BLK:]
                u[o:e, o:] = dot3(inv, s[:, o:], NN)
                if bb > 0:
                    x[o:e, :o] = dot3(inv, s[:, :o], NN)
                if bb < 3:
                    x[o:e, e:] = jnp.zeros((BLK, NB - e), F)
                hook(bb)

        return 0

    lax.fori_loop(0, 4, step, 0)


def factor_kernel(
    diag_in, pt_in, l_ref, x_ref, pr_ref, pc_ref, diag_ref, pt_ref, pack, strip, tb, a_ref, u_ref, s_ref,
    s1, r1, s2, r2, s2b, r2b, sx, rx, sy, ry, sx2, rx2, sy2, ry2, st, s5, r5, s6, r6, own,
):
    r = lax.axis_index("row")
    c = lax.axis_index("col")
    n = 16
    w, m = pt_ref.shape
    z = r // 2
    core = lax.rem(r, 2)
    away = lax.rem(r - c + n, n)
    other = r + 1 - 2 * core
    cy, cx = c // 4, lax.rem(c, 4)
    at = lambda i: pl.ds(pl.multiple_of(i * w, w), w)
    at4 = lambda i: pl.ds(pl.multiple_of(i * 4 * w, 4 * w), 4 * w)
    left, right = pl.ds(0, m // 2), pl.ds(m // 2, m // 2)

    def loop(start, stop, fn):
        def step(t, _):
            fn(t)
            return 0

        lax.fori_loop(start, stop, step, 0)

    def each(count, me, fn):
        loop(1, count, lambda t: fn(lax.rem(me + t, count)))

    fetch = [
        pltpu.make_async_copy(diag_in, diag_ref, own.at[0]),
        pltpu.make_async_copy(pt_in, pt_ref, own.at[1]),
    ]
    for copy in fetch:
        copy.start()
    barrier = pltpu.get_barrier_semaphore()

    def greet(row, col):
        pl.semaphore_signal(barrier, 1, device_id=(row, col), device_id_type=MESH)

    each(n, r, lambda p: greet(p, c))
    each(n, c, lambda p: greet(r, p))
    pl.semaphore_wait(barrier, 2 * (n - 1))

    def remote(src, dst, send, recv, row, col):
        return pltpu.make_async_remote_copy(src, dst, send, recv, device_id=(row, col), device_id_type=MESH)

    def wait_all(part, send, recv, sent):
        every = remote(part, part, send, recv, r, c)
        if sent:
            every.wait_send()
        else:
            every.wait_recv()

    pw = pack.shape[0] // n
    at8 = lambda i: pl.ds(pl.multiple_of(i * pw, pw), pw)

    def diag_copy(src, peer):
        part = pack.at[at8(src), :]
        return remote(part, part, s1, r1, peer, c)

    def strip_copy(src, peer, q):
        part = a_ref.at[at(src), q * BLK :] if q else a_ref.at[at(src), 0:BLK]
        return remote(part, part, s2, r2.at[src], r, peer)

    def rest_copy(src, peer):
        part = a_ref.at[at(src), BLK:]
        return remote(part, part, s2b, r2b.at[src], r, peer)

    def x_first(src, peer):
        return remote(pt_ref.at[:, left], pr_ref.at[at(4 * cy + src), left], sx, rx, r, 4 * cy + peer)

    def y_first(src, peer):
        return remote(pt_ref.at[:, right], pr_ref.at[at(4 * src + cx), right], sy, ry, r, 4 * peer + cx)

    def y_second(src, peer):
        part = pr_ref.at[at4(src), left]
        return remote(part, part, sy2, ry2, r, 4 * peer + cx)

    def x_second(src, peer, j):
        part = pr_ref.at[at(4 * j + src), right]
        return remote(part, part, sx2, rx2, r, 4 * cy + peer)

    def turn_z():
        return remote(pt_ref, tb, st.at[0], st.at[1], lax.rem(r + c, n), c)

    def turn_plane():
        return remote(tb, pc_ref.at[at(c), :], st.at[2], st.at[3], r, away)

    def turn_plane_in():
        return remote(tb, pc_ref.at[at(away), :], st.at[2], st.at[3], r, away)

    def turn_local(src, dst):
        return pltpu.make_async_copy(src, dst, own.at[1])

    def z_row(t):
        return 2 * lax.rem(z + t + 8, 8) + core

    def piece(t, side):
        return pc_ref.at[at(lax.rem(2 * lax.rem(z + t + 8, 8) + side - c + n, n)), :]

    def z_copy(i, src, to):
        part = piece(src, core)
        return remote(part, part, s5, r5.at[(src - to) % 8], z_row(to), c)

    def z_in(src):
        part = piece(src, core)
        return remote(part, part, s5, r5.at[src % 8], r, c)

    def twin_copy(t, side):
        part = piece(t, side)
        return remote(part, part, s6, r6, other, c)

    first = ((0, 2), (0, -2), (0, 1), (0, -1))
    relay = ((-2, 2), (-2, 1), (2, -1))

    fetch[0].wait()
    block = diag_ref[...]
    pack[at8(r), :] = jnp.concatenate([block[pw * j : pw * j + pw, :] for j in range(w // pw)], axis=1)
    each(n, r, lambda p: diag_copy(r, p).start())
    fetch[1].wait()
    keep = pltpu.make_async_copy(pt_ref, pr_ref.at[at(c), :], own.at[0])
    keep.start()

    @pl.when(c != 0)
    def _():
        turn_z().start()

    @pl.when(c == 0)
    def _():
        turn_local(pt_ref, tb).start()

    wait_all(pack.at[0 : (n - 1) * pw], s1, r1, False)
    for i in range(n):
        packed = pack[pw * i : pw * i + pw, :]
        for j in range(w // pw):
            moved = packed if j == 0 else pltpu.roll(packed, BLK - w * j, 1)
            strip[w * i + pw * j : w * i + pw * j + pw, :] = moved[:, :w]
    a_ref[at(c), :] = strip[...].T
    group = c // 4

    def strips(fn, groups):
        for q in groups:

            @pl.when(group == q)
            def _():
                each(n, c, lambda p: fn(p, q))

    strips(lambda p, q: strip_copy(c, p, q).start(), (0,))

    @pl.when(c != 0)
    def _():
        turn_z().wait()

    @pl.when(c == 0)
    def _():
        turn_local(pt_ref, tb).wait()

    @pl.when(away != c)
    def _():
        turn_plane().start()

    @pl.when(away == c)
    def _():
        turn_local(tb, pc_ref.at[at(c), :]).start()

    strips(lambda p, q: rest_copy(c, p).start(), (0,))
    strips(lambda p, q: strip_copy(c, p, q).start(), (1, 2, 3))

    def arrive(bb):
        def one(t):
            @pl.when(t != c)
            def _():
                strip_copy(t, t, bb).wait_recv()

        loop(4 * bb, 4 * bb + 4, one)
        if bb == 0:
            each(4, cx, lambda p: x_first(cx, p).start())
            each(4, cy, lambda p: y_first(cy, p).start())

    def middle(b):
        @pl.when(b == 0)
        def _():
            @pl.when(away != c)
            def _():
                turn_plane_in().wait()

            @pl.when(away == c)
            def _():
                turn_local(tb, pc_ref.at[at(c), :]).wait()

            for i, (src, to) in enumerate(first):
                z_copy(i, src, to).start()
            twin_copy(0, core).start()

        @pl.when(b == 1)
        def _():
            for ready in (-2, 2):
                z_in(ready).wait_recv()
                for i, (src, to) in enumerate(relay):
                    if src == ready:
                        z_copy(4 + i, src, to).start()
                twin_copy(ready, core).start()

        @pl.when(b == 2)
        def _():
            for t in (1, -1):
                z_in(t).wait_recv()
                twin_copy(t, core).start()

        @pl.when(b == 3)
        def _():
            for t in (4, 3, -3):
                z_in(t).wait_recv()
                twin_copy(t, core).start()

    def rest():
        def one(t):
            @pl.when(t != c)
            def _():
                rest_copy(t, t).wait_recv()

        loop(0, 4, one)

    def hook(bb):
        if bb == 0:
            keep.wait()
            wait_all(pr_ref.at[0 : 3 * w, left], sx, rx, False)
            each(4, cy, lambda p: y_second(cy, p).start())
            wait_all(pr_ref.at[0 : 3 * w, right], sy, ry, False)
            for j in range(4):
                each(4, cx, lambda p: x_second(cx, p, j).start())

    factor_blocks(a_ref, u_ref, x_ref, s_ref, arrive, middle, rest, hook)

    rows, cols = l_ref.shape
    per = BLK // w
    chunk = u_ref[at(c), pl.ds(pl.multiple_of((r // per) * BLK, BLK), BLK)]
    turned = pltpu.roll(chunk, lax.rem(BLK - lax.rem(r, per) * w, BLK), 1)[:, :w].T
    gi = r * w + lax.broadcasted_iota(jnp.int32, (rows, cols), 0)
    gj = c * w + lax.broadcasted_iota(jnp.int32, (rows, cols), 1)
    l_ref[...] = jnp.where(gi >= gj, turned, 0.0)

    wait_all(pack.at[0 : (n - 1) * pw], s1, r1, True)
    for q in range(4):

        @pl.when(group == q)
        def _():
            if q == 0:
                wait_all(a_ref.at[0 : (n - 1) * w, 0:BLK], s2, r2.at[0], True)
                wait_all(a_ref.at[0 : (n - 1) * w, BLK:], s2b, r2b.at[0], True)
            else:
                wait_all(a_ref.at[0 : (n - 1) * w, q * BLK :], s2, r2.at[0], True)

    wait_all(pr_ref.at[0 : 3 * w, left], sx, rx, True)
    wait_all(pr_ref.at[0 : 3 * w, right], sy, ry, True)
    wait_all(pc_ref.at[0 : 7 * w, :], s5, r5.at[0], True)
    for sent in (True, False):
        wait_all(pr_ref.at[0 : 12 * w, left], sy2, ry2, sent)
        wait_all(pr_ref.at[0 : 12 * w, right], sx2, rx2, sent)
        wait_all(pc_ref.at[0 : 8 * w, :], s6, r6, sent)


def factor_and_gather(diag, pt):
    w, m = pt.shape
    dma = pltpu.SemaphoreType.DMA
    any_space = pl.BlockSpec(memory_space=pl.ANY)
    vmem = pl.BlockSpec(memory_space=pltpu.VMEM)
    hbm = pl.BlockSpec(memory_space=pltpu.HBM)
    return pl.pallas_call(
        factor_kernel,
        out_shape=(
            jax.ShapeDtypeStruct(diag.shape, F),
            jax.ShapeDtypeStruct((NB, NB), F),
            jax.ShapeDtypeStruct((NB, m), F),
            jax.ShapeDtypeStruct((NB, m), F),
        ),
        in_specs=[hbm, hbm],
        out_specs=[vmem, vmem, any_space, any_space],
        scratch_shapes=[
            pltpu.VMEM(diag.shape, F),
            pltpu.VMEM((w, m), F),
            pltpu.VMEM((w * NB // BLK, BLK), F),
            pltpu.VMEM((NB, w), F),
            pltpu.VMEM((w, m), F),
            pltpu.VMEM((NB, NB), F),
            pltpu.VMEM((NB, NB), F),
            pltpu.VMEM((BLK, NB), F),
        ]
        + [dma(()), dma(()), dma(()), dma((16,)), dma(()), dma((4,)), dma(()), dma(()), dma(()), dma(()), dma(()), dma(()), dma(()), dma(()), dma((4,)), dma(()), dma((8,)), dma(()), dma(()), dma((2,))],
        compiler_params=pltpu.CompilerParams(
            vmem_limit_bytes=40 << 20, collective_id=0, has_side_effects=True
        ),
    )(diag, pt)


STEP = 256


def update_kernel(l_in, x_ref, pr_ref, pc_ref, slab_ref, l_ref, po_ref, out_ref, xc, cc, buf, rows, sem_in, sem_out):
    m, n = buf.shape
    cut = lambda ref, j: ref.at[j * STEP : (j + 1) * STEP]
    steps = range(m // STEP)
    ins = [pltpu.make_async_copy(cut(slab_ref, j), cut(buf, j), sem_in.at[j]) for j in steps]
    outs = [pltpu.make_async_copy(cut(buf, j), cut(out_ref, j), sem_out.at[j]) for j in steps]
    w = po_ref.shape[0]
    mine = rows.at[pl.ds(pl.multiple_of(lax.axis_index("col") * w, w), w)]
    outs.append(pltpu.make_async_copy(l_in, l_ref, sem_out.at[len(ins)]))
    outs.append(pltpu.make_async_copy(mine, po_ref, sem_out.at[len(ins) + 1]))
    for copy in ins:
        copy.start()
    outs[-2].start()

    def dot(a, b):
        return lax.dot_general(a, b, (NN, ((), ())), preferred_element_type=F)

    h, l = split(x_ref[...])
    xc[:, :NB] = h
    xc[:, NB : 2 * NB] = l
    xc[:, 2 * NB :] = h
    h, l = split(pc_ref[...])
    h, l = split(dot(xc[...], jnp.concatenate([h, h, l], axis=0)))
    cc[:NB] = h
    cc[NB : 2 * NB] = h
    cc[2 * NB :] = l
    h, l = split(pr_ref[...])
    rows[...] = dot(xc[...], jnp.concatenate([h, h, l], axis=0))
    outs[-1].start()
    for j in steps:
        h, l = split(rows[:, j * STEP : (j + 1) * STEP].T)
        product = dot(jnp.concatenate([h, l, h], axis=1), cc[...])
        ins[j].wait()
        buf[j * STEP : (j + 1) * STEP] = buf[j * STEP : (j + 1) * STEP] - product
        outs[j].start()
    for copy in outs:
        copy.wait()


def update(factor, x, pr, pc, slab, w):
    m, n = slab.shape
    vmem = pl.BlockSpec(memory_space=pltpu.VMEM)
    any_space = pl.BlockSpec(memory_space=pl.ANY)
    hbm = pl.BlockSpec(memory_space=pltpu.HBM)
    dma = pltpu.SemaphoreType.DMA
    return pl.pallas_call(
        update_kernel,
        out_shape=(
            jax.ShapeDtypeStruct(factor.shape, F),
            jax.ShapeDtypeStruct((w, m), F),
            jax.ShapeDtypeStruct((m, n), F),
        ),
        in_specs=[vmem, vmem, vmem, vmem, hbm],
        out_specs=[hbm, hbm, hbm],
        scratch_shapes=[
            pltpu.VMEM((NB, 3 * NB), jnp.bfloat16),
            pltpu.VMEM((3 * NB, n), jnp.bfloat16),
            pltpu.VMEM((m, n), F),
            pltpu.VMEM((NB, m), F),
            dma((m // STEP,)),
            dma((m // STEP + 2,)),
        ],
        compiler_params=pltpu.CompilerParams(vmem_limit_bytes=48 << 20),
    )(factor, x, pr, pc, slab)


def body(diag_block, panel, slab):
    in_hbm = lambda v: pltpu.with_memory_space_constraint(v, pltpu.HBM)
    factor, inverse, pr, pc = factor_and_gather(in_hbm(diag_block), in_hbm(panel.T))
    factor_out, panel_out, out = update(factor, inverse, pr, pc, slab, panel.shape[1])
    return factor_out, panel_out.T, out


def solution(mesh):
    spec = P("row", "col")
    return jax.shard_map(
        body, mesh=mesh, in_specs=(spec, spec, spec), out_specs=(spec, spec, spec), check_vma=False
    )
```
